1024 devices in a mesh: lat: 128 (over z_lo, x, y), lon: 8 (over z_hi, core).
Axes of the slice: x: 4, y: 8, z: 16 (z_hi: 4, z_lo: 4; z = z_hi * 4 + z_lo), core: 2. Of those that a mesh axis runs over, the one named last changes fastest.
Arguments:
- fields: bfloat16 [512, 576, 256], P('lat', 'lon'), may hold values from -6 to 6
- basis: bfloat16 [512, 25, 9, 25], P('lat'), may hold values from -0.375 to 0.375
- spans: int32 [512, 25], P('lat'), may hold values from 0 to 12, as said below
- weight: bfloat16 [256, 2304], P('lat'), may hold values from -0.125 to 0.125
- cotangent: bfloat16 [512, 576, 256], P('lat', 'lon'), may hold values from -24 to 24
Outputs:
- output: bfloat16 [512, 576, 256], P('lat', 'lon')
- grad_weight: float32 [256, 2304], P('lat')
The draws below stay inside these ranges and needn't reach their ends.
Inputs may be any that keep to these rules, and one draw needn't show every extreme that they name: Rows near the two ends of the band have wider spans.
All inputs are finite; a program needn't handle non-finite values.
Results may differ from the reference program's by a relative error of at most 0.013.
Values may be sent and summed in bfloat16 or wider, within the bound.
No kernel may reach another device: no remote copies, remote signals or barrier semaphores. Data moves between devices by JAX's collectives and lax.ppermute only.
A program may use at most 32 MiB of HBM per device.

```python
import math
import jax
import jax.numpy as jnp
from jax import lax

C = 256
K = 9
RAD = 12
HW = 12
NR = 25
LW = 25
NLAT = 512
NLON = 576


def draw_spans(key, part):
    row_ids = jnp.arange(NLAT)[:, None]
    floor_span = HW * jnp.abs(2 * row_ids - (NLAT - 1)) // (NLAT - 1)
    random_span = jax.random.randint(key, (NLAT, NR), 0, HW + 1)
    return jnp.maximum(random_span, floor_span).astype(jnp.int32)


def spiked(drawn, own_key, source, target, shards_of, factor):
    def block_of(axis_at):
        return (jnp.arange(drawn.shape[axis_at]) // (drawn.shape[axis_at] // shards_of)).reshape((-1,) + (1,) * (drawn.ndim - 1 - axis_at))

    first = jax.random.permutation(own_key, shards_of)[block_of(target)]
    other_side = (block_of(target) + shards_of // 2) % shards_of
    return jnp.where((block_of(source) == first) | (block_of(source) == other_side), factor * drawn, drawn)


def levels(stream_key, shape, pieces, smallest, top_value):
    def one(axis_at, parts):
        heights = jax.random.uniform(jax.random.fold_in(jax.random.fold_in(stream_key, 6), axis_at), (parts,), jnp.float32, smallest / len(pieces), top_value / len(pieces))
        return jnp.repeat(jnp.exp(heights), shape[axis_at] // parts).reshape((-1,) + (1,) * (len(shape) - axis_at - 1))

    loudness = one(*pieces[0])
    for cut in pieces[1:]:
        loudness = loudness * one(*cut)
    return loudness


def gaussian(rng, dims, width, bound, split=(), kind=jnp.bfloat16):
    array = jax.random.normal(rng, dims, jnp.float32) * width
    if len(split) > 0:
        array = levels(rng, dims, split, -0.22, 0.18) * array
    return jnp.clip(array, min=-bound, max=bound).astype(kind)


def gaussian_with(key, extent, scale, most, split, heavy, held_as=jnp.bfloat16):
    drawn = scale * jax.random.normal(key, extent, jnp.float32)
    if split:
        drawn = drawn * levels(key, extent, split, -0.22, 0.18)
    return jnp.clip(spiked(drawn, jax.random.fold_in(key, 3), *heavy), -most, most).astype(held_as)


def setup_inputs(seed: int = 0) -> dict:
    streams_of = jax.random.split(jax.random.key(seed), 6)
    return {
        "fields": gaussian(streams_of[0], (NLAT, NLON, C), 1.0, 6.0, ((0, 128), (1, 8))),
        "basis": gaussian(streams_of[1], (NLAT, NR, K, LW), (NR * HW) ** -0.5, 0.375, ((0, 128),)),
        "spans": draw_spans(jax.random.fold_in(streams_of[5], 71), 0),
        "weight": gaussian(streams_of[3], (C, K * C), (K * C) ** -0.5, 0.125, ((0, 128),)),
        "cotangent": gaussian_with(streams_of[4], (NLAT, NLON, C), 1.0, 24.0, ((0, 128), (1, 8)), (0, 2, 128, 5.5)),
    }


def reference(fields, basis, spans, weight, cotangent):
    offsets = jnp.arange(LW) - HW
    validity = jnp.abs(offsets)[None, None, :] <= spans[:, :, None]
    masked = jnp.where(validity[:, :, None, :], basis.astype(jnp.float32), jnp.float32(0.0))
    wrapped = jnp.concatenate([fields[:, NLON - HW:], fields, fields[:, :HW]], axis=1)
    padded = jnp.pad(wrapped, ((RAD, RAD), (0, 0), (0, 0)))
    weight_t = weight.T
    scale = 1.0 / math.sqrt(NLAT * NLON)

    def step(total, row_index):
        window = lax.dynamic_slice_in_dim(padded, row_index, NR, 0).astype(jnp.float32)
        row_basis = lax.dynamic_index_in_dim(masked, row_index, 0, keepdims=False)
        partial_sums = jnp.einsum('rkw,rvc->kwvc', row_basis, window)
        reduced_total = jnp.zeros((K, NLON, C), jnp.float32)
        for offset in range(LW):
            reduced_total = reduced_total + partial_sums[:, offset, offset:offset + NLON, :]
        features = jnp.transpose(reduced_total, (1, 0, 2)).reshape(NLON, K * C).astype(jnp.bfloat16)
        out_row = jnp.dot(features, weight_t, preferred_element_type=jnp.float32).astype(jnp.bfloat16)
        grad_row = lax.dynamic_index_in_dim(cotangent, row_index, 0, keepdims=False)
        total = total + jnp.dot(grad_row.T, features, preferred_element_type=jnp.float32)
        return (total, out_row)
    total, output = lax.scan(step, jnp.zeros((C, K * C), jnp.float32), jnp.arange(NLAT))
    return (output, total * scale)
```

```python
import math

import jax
import jax.numpy as jnp
from jax import lax
from jax.experimental import pallas as pl
from jax.experimental.pallas import tpu as pltpu
from jax.sharding import PartitionSpec as P

FACTORS = {128: (4, 4, 8), 8: (2, 2, 2)}
TILE = 8


def dot(a, b, contract):
    return lax.dot_general(a, b, (contract, ((), ())), preferred_element_type=jnp.float32)


def lat_index(z, x, y, factors):
    return (z * factors[1] + x) * factors[2] + y


def lat_coords(index, factors):
    return index // (factors[1] * factors[2]), index // factors[2] % factors[1], index % factors[2]


def along(block, dim, step, factors):
    pairs = []
    for source in range(factors[0] * factors[1] * factors[2]):
        coords = list(lat_coords(source, factors))
        coords[dim] = (coords[dim] + step) % factors[dim]
        pairs.append((source, lat_index(*coords, factors)))
    return lax.ppermute(block, "lat", pairs)


def swapped_lat(block, bit):
    return lax.ppermute(block, "lat", [(i, i ^ bit) for i in range(lax.axis_size("lat"))])


def swapped_core(block):
    return lax.ppermute(block, "lon", [(i, i ^ 1) for i in range(lax.axis_size("lon"))])


def along_lon(block, step):
    count = lax.axis_size("lon")
    return lax.ppermute(block, "lon", [(i, (i + step) % count) for i in range(count)])


def passed_along(block, by):
    count = lax.axis_size("lat")
    return lax.ppermute(block, "lat", [(i, i + by) for i in range(count) if 0 <= i + by < count])


def band_kernel(rows_ref, band_ref):
    count, width = rows_ref.shape
    for start in range(0, count, 2):
        pair = []
        for row in (start, start + 1):
            spread = jnp.broadcast_to(rows_ref[row : row + 1, :], (TILE, width))
            pair.append(pltpu.roll(spread, 0, 1, stride=1, stride_axis=0))
        both = jnp.concatenate(pair, axis=0).astype(jnp.bfloat16)
        band_ref[start * TILE : (start + 2) * TILE, :] = both


def feature_kernel(nbasis, tile_count, *refs):
    band_ref, cot_ref = refs[0], refs[1]
    window_refs = refs[2:9]
    features_ref, keep_ref, send_ref = refs[9:]
    rows = window_refs[0].shape[0]
    reach = band_ref.shape[1] // (7 * rows)
    per_tile = rows * TILE
    band = band_ref[...]
    for tile in range(tile_count):
        pieces = []
        for ref in window_refs:
            for row in range(rows):
                pieces.append(ref[row, tile * TILE : tile * TILE + reach, :])
        window = jnp.concatenate(pieces, axis=0)
        summed = dot(band, window, ((1,), (0,))).astype(jnp.bfloat16)
        for k in range(nbasis):
            features_ref[k, tile * per_tile : (tile + 1) * per_tile, :] = summed[
                k * per_tile : (k + 1) * per_tile
            ]
    half = cot_ref.shape[0] // 2
    channels = features_ref.shape[2]
    for k in range(nbasis):
        term = dot(cot_ref[...], features_ref[k], ((1,), (0,)))
        span = slice(k * channels, (k + 1) * channels)
        keep_ref[:, span] = term[:half].astype(keep_ref.dtype)
        send_ref[:, span] = term[half:].astype(send_ref.dtype)


def output_kernel(tile_count, features_ref, weight_ref, order_ref, output_ref):
    nbasis, cells, channels = features_ref.shape
    rows = output_ref.shape[0]
    total = jnp.zeros((cells, weight_ref.shape[0]), jnp.float32)
    for k in range(nbasis):
        piece = weight_ref[:, k * channels : (k + 1) * channels]
        total = total + dot(features_ref[k], piece, ((1,), (1,)))
    mixed = dot(total.astype(jnp.bfloat16), order_ref[...], ((1,), (0,))).astype(jnp.bfloat16)
    for tile in range(tile_count):
        for row in range(rows):
            start = (tile * rows + row) * TILE
            output_ref[row, tile * TILE : (tile + 1) * TILE, :] = mixed[start : start + TILE]


def vmem(count):
    return [pl.BlockSpec(memory_space=pltpu.VMEM)] * count


def shards(fields, basis, spans, weight, cotangent):
    rows, cols, channels = fields.shape
    extent, nbasis, width = basis.shape[1:]
    outs = cotangent.shape[2]
    reach = (width - 1) // 2
    factors = FACTORS[lax.axis_size("lat")]
    lat = lax.axis_index("lat")
    lon = lax.axis_index("lon")
    core = lon % 2
    z_at, x_at, y_at = lat_coords(lat, factors)
    tile_count = cols // TILE
    window_rows = extent + rows - 1
    window_cols = TILE + width - 1
    cells = rows * cols
    bf16 = jnp.bfloat16

    left = along_lon(fields[:, cols - reach :], 1)
    right = along_lon(fields[:, :reach], -1)
    own = jnp.concatenate([left, fields, right], axis=1)
    below, above = [own], [own]
    for _ in range(3):
        below.append(passed_along(below[-1], 1))
        above.append(passed_along(above[-1], -1))
    windows = below[:0:-1] + [own] + above[1:]

    gathered = lax.dynamic_slice_in_dim(weight, core, 1, 0)
    bit = 1
    while bit < lax.axis_size("lat"):
        gathered = jnp.concatenate([gathered, swapped_lat(gathered, bit)], axis=0)
        bit *= 2
    all_weight = jnp.concatenate([gathered, swapped_core(gathered)], axis=0)
    position = jnp.arange(outs)
    half = outs // 2
    weight_row = 2 * (lat ^ (position % half)) + (core ^ (position // half))
    weight_order = (weight_row[:, None] == jnp.arange(outs)[None, :]).astype(bf16)

    offsets = jnp.arange(width) - reach
    validity = jnp.abs(offsets)[None, None, :] <= spans[:, :, None]
    masked = jnp.where(validity[:, :, None, :], basis, jnp.zeros_like(basis))
    masked = jnp.transpose(masked, (2, 0, 1, 3)).astype(jnp.float32)
    band_rows = jnp.stack(
        [
            jnp.pad(masked[:, row], ((0, 0), (row, rows - 1 - row), (0, window_cols - width)))
            for row in range(rows)
        ],
        axis=1,
    ).reshape(nbasis * rows, window_rows * window_cols)
    band = pl.pallas_call(
        band_kernel,
        out_shape=jax.ShapeDtypeStruct((nbasis * rows * TILE, window_rows * window_cols), bf16),
        in_specs=vmem(1),
        out_specs=pl.BlockSpec(memory_space=pltpu.VMEM),
    )(band_rows)

    zs, xs, ys = factors
    away = (
        2
        * lat_index(
            (z_at + position // ys % zs) % zs,
            (x_at + position // (ys * zs) % xs) % xs,
            (y_at + position % ys) % ys,
            factors,
        )
        + (core ^ (position // half))
    )
    cot_order = (away[:, None] == jnp.arange(outs)[None, :]).astype(bf16)
    cot_cells = jnp.transpose(cotangent.reshape(rows, tile_count, TILE, outs), (1, 0, 2, 3))
    cot = dot(cot_order, cot_cells.reshape(cells, outs), ((1,), (1,))).astype(bf16)

    features, keep, send = pl.pallas_call(
        lambda *refs: feature_kernel(nbasis, tile_count, *refs),
        out_shape=(
            jax.ShapeDtypeStruct((nbasis, cells, channels), bf16),
            jax.ShapeDtypeStruct((half, nbasis * channels), bf16),
            jax.ShapeDtypeStruct((half, nbasis * channels), bf16),
        ),
        in_specs=vmem(9),
        out_specs=tuple(vmem(3)),
        name="features",
    )(band, cot, *windows)

    output = pl.pallas_call(
        lambda *refs: output_kernel(tile_count, *refs),
        out_shape=jax.ShapeDtypeStruct((rows, cols, outs), bf16),
        in_specs=vmem(3),
        out_specs=pl.BlockSpec(memory_space=pltpu.VMEM),
        name="mixing",
    )(features, all_weight, weight_order)

    f32 = jnp.float32
    total = keep.astype(f32) + swapped_core(send).astype(f32)
    for dim in (1, 0, 2):
        count = factors[dim]
        piece = total.shape[0] // count
        moved = total if dim == 2 else total.astype(bf16)
        arrived = [
            along(moved[step * piece : (step + 1) * piece], dim, step, factors)
            for step in range(1, count)
        ]
        total = total[:piece]
        for part in arrived:
            total = total + part.astype(f32)
    hi = lax.axis_size("lon") // 2
    if hi == 4:
        one, two, three = (along_lon(total, 2 * step) for step in (1, 2, 3))
        total = (total + two) + (one + three)
    scale = 1.0 / math.sqrt(rows * lax.axis_size("lat") * cols * lax.axis_size("lon"))
    total = total * scale
    other = swapped_core(total)
    grad_weight = jnp.where(
        core == 0,
        jnp.concatenate([total, other], axis=0),
        jnp.concatenate([other, total], axis=0),
    )
    return (output, grad_weight)


def solution(mesh):
    return jax.shard_map(
        shards,
        mesh=mesh,
        in_specs=(
            P("lat", "lon", None),
            P("lat", None, None, None),
            P("lat", None),
            P("lat", None),
            P("lat", "lon", None),
        ),
        out_specs=(P("lat", "lon", None), P("lat", None)),
        check_vma=False,
    )
```

```python
import math

import jax
import jax.numpy as jnp
from jax import lax
from jax.experimental import pallas as pl
from jax.experimental.pallas import tpu as pltpu
from jax.sharding import PartitionSpec as P

FACTORS = {128: (4, 4, 8), 8: (2, 2, 2)}
TILE = 8
MASKS = {128: (8, 16, 32, 64, 1, 2, 7), 8: (2, 4, 1)}


def dot(a, b, contract):
    return lax.dot_general(a, b, (contract, ((), ())), preferred_element_type=jnp.float32)


def lat_index(z, x, y, factors):
    return (z * factors[1] + x) * factors[2] + y


def lat_coords(index, factors):
    return index // (factors[1] * factors[2]), index // factors[2] % factors[1], index % factors[2]


def groups(dims, factors):
    members = {}
    for index in range(factors[0] * factors[1] * factors[2]):
        coords = lat_coords(index, factors)
        fixed = tuple(coords[d] for d in range(3) if d not in dims)
        members.setdefault(fixed, []).append(index)
    return [members[fixed] for fixed in sorted(members)]


def swapped_lat(block, bit):
    return lax.ppermute(block, "lat", [(i, i ^ bit) for i in range(lax.axis_size("lat"))])


def swapped_core(block):
    return lax.ppermute(block, "lon", [(i, i ^ 1) for i in range(lax.axis_size("lon"))])


def paired(block, axis, first, loop):
    count = lax.axis_size(axis)
    pairs = []
    for low in range(first, count, 2):
        high = low + 1
        if high == count:
            if not loop:
                continue
            high = 0
        pairs += [(low, high), (high, low)]
    return lax.ppermute(block, axis, pairs)


def band_kernel(rows_ref, band_ref):
    count, width = rows_ref.shape
    for start in range(0, count, 2):
        pair = []
        for row in (start, start + 1):
            spread = jnp.broadcast_to(rows_ref[row : row + 1, :], (TILE, width))
            pair.append(pltpu.roll(spread, 0, 1, stride=1, stride_axis=0))
        both = jnp.concatenate(pair, axis=0).astype(jnp.bfloat16)
        band_ref[start * TILE : (start + 2) * TILE, :] = both


def feature_kernel(nbasis, tile_count, *refs):
    band_ref, cot_ref = refs[0], refs[1]
    window_refs = refs[2:9]
    features_ref, keep_ref, send_ref = refs[9:]
    rows = window_refs[0].shape[0]
    reach = band_ref.shape[1] // (7 * rows)
    per_tile = rows * TILE
    band = band_ref[...]
    for tile in range(tile_count):
        pieces = []
        for ref in window_refs:
            for row in range(rows):
                pieces.append(ref[row, tile * TILE : tile * TILE + reach, :])
        window = jnp.concatenate(pieces, axis=0)
        summed = dot(band, window, ((1,), (0,))).astype(jnp.bfloat16)
        for k in range(nbasis):
            features_ref[k, tile * per_tile : (tile + 1) * per_tile, :] = summed[
                k * per_tile : (k + 1) * per_tile
            ]
    half = cot_ref.shape[0] // 2
    channels = features_ref.shape[2]
    for k in range(nbasis):
        term = dot(cot_ref[...], features_ref[k], ((1,), (0,)))
        span = slice(k * channels, (k + 1) * channels)
        keep_ref[:, span] = term[:half].astype(keep_ref.dtype)
        send_ref[:, span] = term[half:].astype(send_ref.dtype)


def output_kernel(tile_count, features_ref, mine_ref, other_ref, order_ref, output_ref):
    nbasis, cells, channels = features_ref.shape
    rows = output_ref.shape[0]
    total = jnp.zeros((cells, order_ref.shape[0]), jnp.float32)
    for k in range(nbasis):
        span = slice(k * channels, (k + 1) * channels)
        piece = jnp.concatenate([mine_ref[:, span], other_ref[:, span]], axis=0)
        total = total + dot(features_ref[k], piece, ((1,), (1,)))
    mixed = dot(total.astype(jnp.bfloat16), order_ref[...], ((1,), (0,))).astype(jnp.bfloat16)
    for tile in range(tile_count):
        for row in range(rows):
            start = (tile * rows + row) * TILE
            output_ref[row, tile * TILE : (tile + 1) * TILE, :] = mixed[start : start + TILE]


def vmem(count):
    return [pl.BlockSpec(memory_space=pltpu.VMEM)] * count


def shards(fields, basis, spans, weight, cotangent):
    rows, cols, channels = fields.shape
    extent, nbasis, width = basis.shape[1:]
    outs = cotangent.shape[2]
    reach = (width - 1) // 2
    factors = FACTORS[lax.axis_size("lat")]
    lat = lax.axis_index("lat")
    lon = lax.axis_index("lon")
    core = lon % 2
    tile_count = cols // TILE
    window_rows = extent + rows - 1
    window_cols = TILE + width - 1
    cells = rows * cols
    bf16 = jnp.bfloat16

    masks = MASKS[lax.axis_size("lat")]
    owners = [0]
    for mask in masks:
        owners = owners + [owner ^ mask for owner in owners]

    def doubled(block, turn):
        if turn >= len(masks):
            return block
        return jnp.concatenate([block, swapped_lat(block, masks[turn])], axis=0)

    gathered = doubled(lax.dynamic_slice_in_dim(weight, core, 1, 0), 0)

    edges = jnp.where(core == 0, fields[:, cols - reach :], fields[:, :reach])
    other_edges = jnp.where(core == 0, fields[:, :reach], fields[:, cols - reach :])
    near_edge = paired(edges, "lon", 0, True)
    far_edge = paired(other_edges, "lon", 1, True)
    left = jnp.where(core == 0, far_edge, near_edge)
    right = jnp.where(core == 0, near_edge, far_edge)
    own = jnp.concatenate([left, fields, right], axis=1)
    near, far = own, own
    nears, fars = [], []
    for turn in range(3):
        near, far, gathered = lax.optimization_barrier((near, far, gathered))
        near, far = paired(far, "lat", 0, False), paired(near, "lat", 1, False)
        gathered = doubled(gathered, turn + 1)
        nears.append(near)
        fars.append(far)
    windows = nears[::-1] + [own] + fars

    near, gathered = lax.optimization_barrier((near, gathered))
    nears[-1] = near
    for turn in range(4, len(masks)):
        gathered = doubled(gathered, turn)
    other_weight = swapped_core(gathered)
    position = jnp.arange(outs)
    half = outs // 2
    weight_row = 2 * (lat ^ jnp.array(owners + owners, jnp.int32)) + (core ^ (position // half))
    weight_order = (weight_row[:, None] == jnp.arange(outs)[None, :]).astype(bf16)

    offsets = jnp.arange(width) - reach
    validity = jnp.abs(offsets)[None, None, :] <= spans[:, :, None]
    masked = jnp.where(validity[:, :, None, :], basis, jnp.zeros_like(basis))
    masked = jnp.transpose(masked, (2, 0, 1, 3)).astype(jnp.float32)
    band_rows = jnp.stack(
        [
            jnp.pad(masked[:, row], ((0, 0), (row, rows - 1 - row), (0, window_cols - width)))
            for row in range(rows)
        ],
        axis=1,
    ).reshape(nbasis * rows, window_rows // rows, rows * window_cols)
    band_rows = jnp.where(lat % 2 == 0, band_rows[:, ::-1], band_rows)
    band_rows = band_rows.reshape(nbasis * rows, window_rows * window_cols)
    band = pl.pallas_call(
        band_kernel,
        out_shape=jax.ShapeDtypeStruct((nbasis * rows * TILE, window_rows * window_cols), bf16),
        in_specs=vmem(1),
        out_specs=pl.BlockSpec(memory_space=pltpu.VMEM),
    )(band_rows)

    zs, xs, ys = factors
    away = (
        2
        * lat_index(
            position // ys % zs, position // (ys * zs) % xs, position % ys, factors
        )
        + (core ^ (position // half))
    )
    cot_order = (away[:, None] == jnp.arange(outs)[None, :]).astype(bf16)
    cot_cells = jnp.transpose(cotangent.reshape(rows, tile_count, TILE, outs), (1, 0, 2, 3))
    cot = dot(cot_order, cot_cells.reshape(cells, outs), ((1,), (1,))).astype(bf16)

    features, keep, send = pl.pallas_call(
        lambda *refs: feature_kernel(nbasis, tile_count, *refs),
        out_shape=(
            jax.ShapeDtypeStruct((nbasis, cells, channels), bf16),
            jax.ShapeDtypeStruct((half, nbasis * channels), bf16),
            jax.ShapeDtypeStruct((half, nbasis * channels), bf16),
        ),
        in_specs=vmem(9),
        out_specs=tuple(vmem(3)),
        name="features",
    )(band, cot, *windows)

    output = pl.pallas_call(
        lambda *refs: output_kernel(tile_count, *refs),
        out_shape=jax.ShapeDtypeStruct((rows, cols, outs), bf16),
        in_specs=vmem(4),
        out_specs=pl.BlockSpec(memory_space=pltpu.VMEM),
        name="mixing",
    )(features, gathered, other_weight, weight_order)

    f32 = jnp.float32
    total = keep.astype(f32) + swapped_core(send).astype(f32)
    for dim in (1, 0, 2):
        count = factors[dim]
        moved = total if dim == 2 else total.astype(bf16)
        moved = moved.reshape(count, -1, moved.shape[1])
        arrived = lax.all_to_all(moved, "lat", 0, 0, axis_index_groups=groups((dim,), factors))
        total = jnp.sum(arrived.astype(f32), axis=0)
    scale = 1.0 / math.sqrt(rows * lax.axis_size("lat") * cols * lax.axis_size("lon"))
    lon_size = lax.axis_size("lon")
    spread = jnp.broadcast_to(total * scale, (lon_size,) + total.shape)
    arrived = lax.all_to_all(spread, "lon", 0, 0)
    grad_weight = jnp.sum(arrived.reshape(lon_size // 2, 2, nbasis * channels), axis=0)
    return (output, grad_weight)


def solution(mesh):
    return jax.shard_map(
        shards,
        mesh=mesh,
        in_specs=(
            P("lat", "lon", None),
            P("lat", None, None, None),
            P("lat", None),
            P("lat", None),
            P("lat", "lon", None),
        ),
        out_specs=(P("lat", "lon", None), P("lat", None)),
        check_vma=False,
    )
```

```python
import math

import jax
import jax.numpy as jnp
from jax import lax
from jax.experimental import pallas as pl
from jax.experimental.pallas import tpu as pltpu
from jax.sharding import PartitionSpec as P

FACTORS = {128: (4, 4, 8), 8: (2, 2, 2)}
TILE = 8


def dot(a, b, contract):
    return lax.dot_general(a, b, (contract, ((), ())), preferred_element_type=jnp.float32)


def lat_index(z, x, y, factors):
    return (z * factors[1] + x) * factors[2] + y


def lat_coords(index, factors):
    return index // (factors[1] * factors[2]), index // factors[2] % factors[1], index % factors[2]


def groups(dims, factors):
    members = {}
    for index in range(factors[0] * factors[1] * factors[2]):
        coords = lat_coords(index, factors)
        fixed = tuple(coords[d] for d in range(3) if d not in dims)
        members.setdefault(fixed, []).append(index)
    return [members[fixed] for fixed in sorted(members)]


def swapped_core(block):
    return lax.ppermute(block, "lon", [(i, i ^ 1) for i in range(lax.axis_size("lon"))])


def passed_along(block, by):
    count = lax.axis_size("lat")
    return lax.ppermute(block, "lat", [(i, i + by) for i in range(count) if 0 <= i + by < count])


def paired(block, axis, first, loop):
    count = lax.axis_size(axis)
    pairs = []
    for low in range(first, count, 2):
        high = low + 1
        if high == count:
            if not loop:
                continue
            high = 0
        pairs += [(low, high), (high, low)]
    return lax.ppermute(block, axis, pairs)


def spread_over(block, dim, factors):
    copies = jnp.broadcast_to(block, (factors[dim],) + block.shape)
    joined = lax.all_to_all(copies, "lat", 0, 0, axis_index_groups=groups((dim,), factors))
    return joined.reshape(-1, block.shape[1])


def doubled(block, mask, factors):
    mask = mask * factors[1] * factors[2]
    pairs = [(i, i ^ mask) for i in range(lax.axis_size("lat"))]
    return jnp.concatenate([block, lax.ppermute(block, "lat", pairs)], axis=0)


def band_kernel(rows_ref, band_ref):
    count, width = rows_ref.shape
    for start in range(0, count, 2):
        pair = []
        for row in (start, start + 1):
            spread = jnp.broadcast_to(rows_ref[row : row + 1, :], (TILE, width))
            pair.append(pltpu.roll(spread, 0, 1, stride=1, stride_axis=0))
        both = jnp.concatenate(pair, axis=0).astype(jnp.bfloat16)
        band_ref[start * TILE : (start + 2) * TILE, :] = both


def feature_kernel(nbasis, tile_count, core_ref, band_ref, cot_ref, near_ref, far_ref, *refs):
    piece_refs = refs[:7]
    features_ref, keep_ref, send_ref, window_ref = refs[7:]
    rows, cols, _ = piece_refs[0].shape
    window_rows = window_ref.shape[0]
    reach = near_ref.shape[1]
    span = band_ref.shape[1] // window_rows
    per_tile = rows * TILE
    first = core_ref[0] == 0
    for row in range(window_rows):
        near, far = near_ref[row], far_ref[row]
        window_ref[row, :reach, :] = jnp.where(first, far, near)
        window_ref[row, reach : reach + cols, :] = piece_refs[row // rows][row % rows]
        window_ref[row, reach + cols :, :] = jnp.where(first, near, far)
    band = band_ref[...]
    for tile in range(tile_count):
        window = window_ref[:, tile * TILE : tile * TILE + span, :]
        window = window.reshape(window_rows * span, window.shape[2])
        summed = dot(band, window, ((1,), (0,))).astype(jnp.bfloat16)
        for k in range(nbasis):
            features_ref[k, tile * per_tile : (tile + 1) * per_tile, :] = summed[
                k * per_tile : (k + 1) * per_tile
            ]
    half = cot_ref.shape[0] // 2
    channels = features_ref.shape[2]
    for k in range(nbasis):
        term = dot(cot_ref[...], features_ref[k], ((1,), (0,)))
        span = slice(k * channels, (k + 1) * channels)
        keep_ref[:, span] = term[:half].astype(keep_ref.dtype)
        send_ref[:, span] = term[half:].astype(send_ref.dtype)


def output_kernel(tile_count, features_ref, mine_ref, other_ref, order_ref, output_ref):
    nbasis, cells, channels = features_ref.shape
    rows = output_ref.shape[0]
    total = jnp.zeros((cells, order_ref.shape[0]), jnp.float32)
    for k in range(nbasis):
        span = slice(k * channels, (k + 1) * channels)
        piece = jnp.concatenate([mine_ref[:, span], other_ref[:, span]], axis=0)
        total = total + dot(features_ref[k], piece, ((1,), (1,)))
    mixed = dot(total.astype(jnp.bfloat16), order_ref[...], ((1,), (0,))).astype(jnp.bfloat16)
    for tile in range(tile_count):
        for row in range(rows):
            start = (tile * rows + row) * TILE
            output_ref[row, tile * TILE : (tile + 1) * TILE, :] = mixed[start : start + TILE]


def vmem(count):
    return [pl.BlockSpec(memory_space=pltpu.VMEM)] * count


def shards(fields, basis, spans, weight, cotangent):
    rows, cols, channels = fields.shape
    extent, nbasis, width = basis.shape[1:]
    outs = cotangent.shape[2]
    reach = (width - 1) // 2
    factors = FACTORS[lax.axis_size("lat")]
    lat = lax.axis_index("lat")
    lon = lax.axis_index("lon")
    core = lon % 2
    tile_count = cols // TILE
    window_rows = extent + rows - 1
    window_cols = TILE + width - 1
    cells = rows * cols
    bf16 = jnp.bfloat16

    gathered = lax.dynamic_slice_in_dim(weight, core, 1, 0)
    gathered = spread_over(gathered, 2, factors)
    gathered = doubled(gathered, 1, factors)
    gathered = spread_over(gathered, 1, factors)

    offsets = jnp.arange(width) - reach
    validity = jnp.abs(offsets)[None, None, :] <= spans[:, :, None]
    masked = jnp.where(validity[:, :, None, :], basis, jnp.zeros_like(basis))
    masked = jnp.transpose(masked, (2, 0, 1, 3)).astype(jnp.float32)
    band_rows = jnp.stack(
        [
            jnp.pad(masked[:, row], ((0, 0), (row, rows - 1 - row), (0, window_cols - width)))
            for row in range(rows)
        ],
        axis=1,
    ).reshape(nbasis * rows, window_rows * window_cols)
    band = pl.pallas_call(
        band_kernel,
        out_shape=jax.ShapeDtypeStruct((nbasis * rows * TILE, window_rows * window_cols), bf16),
        in_specs=vmem(1),
        out_specs=pl.BlockSpec(memory_space=pltpu.VMEM),
    )(band_rows)

    zs, xs, ys = factors
    z_at = lat // (xs * ys)
    position = jnp.arange(outs)
    half = outs // 2
    away = (
        2
        * lat_index(
            position // ys % zs, position // (ys * zs) % xs, position % ys, factors
        )
        + (core ^ (position // half))
    )
    cot_order = (away[:, None] == jnp.arange(outs)[None, :]).astype(bf16)
    cot_cells = jnp.transpose(cotangent.reshape(rows, tile_count, TILE, outs), (1, 0, 2, 3))
    cot = dot(cot_order, cot_cells.reshape(cells, outs), ((1,), (1,))).astype(bf16)

    shifts = (3, 2, 1, -1, -2, -3)
    windows = {0: fields}
    for by in shifts:
        windows[by] = passed_along(fields, by)
    pieces = [windows[by] for by in (3, 2, 1, 0, -1, -2, -3)]
    low = jnp.concatenate([piece[:, :reach] for piece in pieces], axis=0)
    high = jnp.concatenate([piece[:, cols - reach :] for piece in pieces], axis=0)
    to_near = jnp.where(core == 0, high, low)
    to_far = jnp.where(core == 0, low, high)
    to_near, to_far, band, cot, gathered = lax.optimization_barrier(
        (to_near, to_far, band, cot, gathered)
    )
    far_edge = paired(to_far, "lon", 1, True)
    near_edge = paired(to_near, "lon", 0, True)

    features, keep, send = pl.pallas_call(
        lambda *refs: feature_kernel(nbasis, tile_count, *refs),
        out_shape=(
            jax.ShapeDtypeStruct((nbasis, cells, channels), bf16),
            jax.ShapeDtypeStruct((half, nbasis * channels), bf16),
            jax.ShapeDtypeStruct((half, nbasis * channels), bf16),
        ),
        in_specs=[pl.BlockSpec(memory_space=pltpu.SMEM)] + vmem(11),
        out_specs=tuple(vmem(3)),
        scratch_shapes=[pltpu.VMEM((window_rows, cols + 2 * reach, channels), bf16)],
        name="features",
    )(core.reshape(1).astype(jnp.int32), band, cot, near_edge, far_edge, *pieces)

    if zs == 4:
        gathered = doubled(gathered, 2, factors)
    place = position % half
    from_z = z_at ^ (place // ys % 2 + place // (2 * ys * xs) * 2)
    weight_row = 2 * lat_index(from_z, place // (2 * ys) % xs, place % ys, factors)
    weight_row = weight_row + (core ^ (position // half))
    weight_order = (weight_row[:, None] == jnp.arange(outs)[None, :]).astype(bf16)

    f32 = jnp.float32
    total = keep.astype(f32) + swapped_core(send).astype(f32)
    for dim in (1, 0, 2):
        count = factors[dim]
        if dim == 0:
            total, gathered = lax.optimization_barrier((total, gathered))
        moved = total if dim == 2 else total.astype(bf16)
        moved = moved.reshape(count, -1, moved.shape[1])
        arrived = lax.all_to_all(moved, "lat", 0, 0, axis_index_groups=groups((dim,), factors))
        total = jnp.sum(arrived.astype(f32), axis=0)
    other_weight = swapped_core(gathered)
    output = pl.pallas_call(
        lambda *refs: output_kernel(tile_count, *refs),
        out_shape=jax.ShapeDtypeStruct((rows, cols, outs), bf16),
        in_specs=vmem(4),
        out_specs=pl.BlockSpec(memory_space=pltpu.VMEM),
        name="mixing",
    )(features, gathered, other_weight, weight_order)

    scale = 1.0 / math.sqrt(rows * lax.axis_size("lat") * cols * lax.axis_size("lon"))
    lon_size = lax.axis_size("lon")
    spread = jnp.broadcast_to(total * scale, (lon_size,) + total.shape)
    arrived = lax.all_to_all(spread, "lon", 0, 0)
    grad_weight = jnp.sum(arrived.reshape(lon_size // 2, 2, nbasis * channels), axis=0)
    return (output, grad_weight)


def solution(mesh):
    return jax.shard_map(
        shards,
        mesh=mesh,
        in_specs=(
            P("lat", "lon", None),
            P("lat", None, None, None),
            P("lat", None),
            P("lat", None),
            P("lat", "lon", None),
        ),
        out_specs=(P("lat", "lon", None), P("lat", None)),
        check_vma=False,
    )
```

```python
import math

import jax
import jax.numpy as jnp
from jax import lax
from jax.experimental import pallas as pl
from jax.experimental.pallas import tpu as pltpu
from jax.sharding import PartitionSpec as P

FACTORS = {128: (4, 4, 8), 16: (2, 2, 4)}
TILE = 8


def dot(a, b, contract):
    return lax.dot_general(a, b, (contract, ((), ())), preferred_element_type=jnp.float32)


def lat_index(z, x, y, factors):
    return (z * factors[1] + x) * factors[2] + y


def lat_coords(index, factors):
    return index // (factors[1] * factors[2]), index // factors[2] % factors[1], index % factors[2]


def groups(dims, factors):
    members = {}
    for index in range(factors[0] * factors[1] * factors[2]):
        coords = lat_coords(index, factors)
        fixed = tuple(coords[d] for d in range(3) if d not in dims)
        members.setdefault(fixed, []).append(index)
    return [members[fixed] for fixed in sorted(members)]


def swapped_core(block):
    return lax.ppermute(block, "lon", [(i, i ^ 1) for i in range(lax.axis_size("lon"))])


def paired(block, axis, first, loop):
    count = lax.axis_size(axis)
    pairs = []
    for low in range(first, count, 2):
        high = low + 1
        if high == count:
            if not loop:
                continue
            high = 0
        pairs += [(low, high), (high, low)]
    return lax.ppermute(block, axis, pairs)


def spread_over(block, dim, factors):
    copies = jnp.broadcast_to(block, (factors[dim],) + block.shape)
    joined = lax.all_to_all(copies, "lat", 0, 0, axis_index_groups=groups((dim,), factors))
    return joined.reshape(-1, block.shape[1])


def band_kernel(rows_ref, band_ref):
    count, width = rows_ref.shape
    for start in range(0, count, 2):
        pair = []
        for row in (start, start + 1):
            spread = jnp.broadcast_to(rows_ref[row : row + 1, :], (TILE, width))
            pair.append(pltpu.roll(spread, 0, 1, stride=1, stride_axis=0))
        both = jnp.concatenate(pair, axis=0).astype(jnp.bfloat16)
        band_ref[start * TILE : (start + 2) * TILE, :] = both


def feature_kernel(nbasis, tile_count, *refs):
    band_ref, cot_ref = refs[0], refs[1]
    window_refs = refs[2:9]
    features_ref, keep_ref, send_ref = refs[9:]
    rows = window_refs[0].shape[0]
    reach = band_ref.shape[1] // (7 * rows)
    per_tile = rows * TILE
    band = band_ref[...]
    for tile in range(tile_count):
        pieces = []
        for ref in window_refs:
            for row in range(rows):
                pieces.append(ref[row, tile * TILE : tile * TILE + reach, :])
        window = jnp.concatenate(pieces, axis=0)
        summed = dot(band, window, ((1,), (0,))).astype(jnp.bfloat16)
        for k in range(nbasis):
            features_ref[k, tile * per_tile : (tile + 1) * per_tile, :] = summed[
                k * per_tile : (k + 1) * per_tile
            ]
    half = cot_ref.shape[0] // 2
    channels = features_ref.shape[2]
    for k in range(nbasis):
        term = dot(cot_ref[...], features_ref[k], ((1,), (0,)))
        span = slice(k * channels, (k + 1) * channels)
        keep_ref[:, span] = term[:half].astype(keep_ref.dtype)
        send_ref[:, span] = term[half:].astype(send_ref.dtype)


def output_kernel(tile_count, features_ref, mine_ref, other_ref, order_ref, output_ref):
    nbasis, cells, channels = features_ref.shape
    rows = output_ref.shape[0]
    total = jnp.zeros((cells, order_ref.shape[0]), jnp.float32)
    for k in range(nbasis):
        span = slice(k * channels, (k + 1) * channels)
        piece = jnp.concatenate([mine_ref[:, span], other_ref[:, span]], axis=0)
        total = total + dot(features_ref[k], piece, ((1,), (1,)))
    mixed = dot(total.astype(jnp.bfloat16), order_ref[...], ((1,), (0,))).astype(jnp.bfloat16)
    for tile in range(tile_count):
        for row in range(rows):
            start = (tile * rows + row) * TILE
            output_ref[row, tile * TILE : (tile + 1) * TILE, :] = mixed[start : start + TILE]


def vmem(count):
    return [pl.BlockSpec(memory_space=pltpu.VMEM)] * count


def shards(fields, basis, spans, weight, cotangent):
    rows, cols, channels = fields.shape
    extent, nbasis, width = basis.shape[1:]
    outs = cotangent.shape[2]
    reach = (width - 1) // 2
    factors = FACTORS[lax.axis_size("lat")]
    lat = lax.axis_index("lat")
    lon = lax.axis_index("lon")
    core = lon % 2
    tile_count = cols // TILE
    window_rows = extent + rows - 1
    window_cols = TILE + width - 1
    cells = rows * cols
    bf16 = jnp.bfloat16

    gathered = spread_over(lax.dynamic_slice_in_dim(weight, core, 1, 0), 1, factors)

    offsets = jnp.arange(width) - reach
    validity = jnp.abs(offsets)[None, None, :] <= spans[:, :, None]
    masked = jnp.where(validity[:, :, None, :], basis, jnp.zeros_like(basis))
    masked = jnp.transpose(masked, (2, 0, 1, 3)).astype(jnp.float32)
    band_rows = jnp.stack(
        [
            jnp.pad(masked[:, row], ((0, 0), (row, rows - 1 - row), (0, window_cols - width)))
            for row in range(rows)
        ],
        axis=1,
    ).reshape(nbasis * rows, window_rows // rows, rows * window_cols)
    band_rows = jnp.where(lat % 2 == 0, band_rows[:, ::-1], band_rows)
    band_rows = band_rows.reshape(nbasis * rows, window_rows * window_cols)
    band = pl.pallas_call(
        band_kernel,
        out_shape=jax.ShapeDtypeStruct((nbasis * rows * TILE, window_rows * window_cols), bf16),
        in_specs=vmem(1),
        out_specs=pl.BlockSpec(memory_space=pltpu.VMEM),
    )(band_rows)

    zs, xs, ys = factors
    position = jnp.arange(outs)
    half = outs // 2
    away = (
        2
        * lat_index(
            position // ys % zs, position // (ys * zs) % xs, position % ys, factors
        )
        + (core ^ (position // half))
    )
    cot_order = (away[:, None] == jnp.arange(outs)[None, :]).astype(bf16)
    cot_cells = jnp.transpose(cotangent.reshape(rows, tile_count, TILE, outs), (1, 0, 2, 3))
    cot = dot(cot_order, cot_cells.reshape(cells, outs), ((1,), (1,))).astype(bf16)

    low, high = fields[:, :reach], fields[:, cols - reach :]
    near_edge = paired(jnp.where(core == 0, high, low), "lon", 0, True)
    far_edge = paired(jnp.where(core == 0, low, high), "lon", 1, True)
    left = jnp.where(core == 0, far_edge, near_edge)
    right = jnp.where(core == 0, near_edge, far_edge)
    own = jnp.concatenate([left, fields, right], axis=1)
    own, gathered = lax.optimization_barrier((own, gathered))
    near, far = own, own
    nears, fars = [], []
    for turn in range(3):
        if turn == 2:
            near, far, band, cot = lax.optimization_barrier((near, far, band, cot))
        near, far = paired(far, "lat", 0, False), paired(near, "lat", 1, False)
        nears.append(near)
        fars.append(far)
    windows = nears[::-1] + [own] + fars

    features, keep, send = pl.pallas_call(
        lambda *refs: feature_kernel(nbasis, tile_count, *refs),
        out_shape=(
            jax.ShapeDtypeStruct((nbasis, cells, channels), bf16),
            jax.ShapeDtypeStruct((half, nbasis * channels), bf16),
            jax.ShapeDtypeStruct((half, nbasis * channels), bf16),
        ),
        in_specs=vmem(9),
        out_specs=tuple(vmem(3)),
        name="features",
    )(band, cot, *windows)

    f32 = jnp.float32
    length = nbasis * channels

    def exchanged(block, dim):
        block = block.reshape(factors[dim], -1, block.shape[-1])
        return lax.all_to_all(block, "lat", 0, 0, axis_index_groups=groups((dim,), factors))

    total = (keep.astype(f32) + swapped_core(send).astype(f32)).astype(bf16)
    total = jnp.sum(exchanged(total, 1).astype(f32), axis=0).astype(bf16)

    total = total.reshape(zs, ys, length)
    folded = jnp.concatenate([gathered[:, : length // 2], gathered[:, length // 2 :]], axis=0)
    folded = jnp.pad(folded, ((0, ys - folded.shape[0]), (0, 0)))
    folded = jnp.broadcast_to(folded, (zs,) + folded.shape)
    arrived = exchanged(jnp.concatenate([total, folded], axis=2), 0)
    total = jnp.sum(arrived[:, :, :length].astype(f32), axis=0).astype(bf16)
    gathered = jnp.concatenate(
        [arrived[:, :xs, length:], arrived[:, xs : 2 * xs, length:]], axis=2
    ).reshape(zs * xs, length)

    piece = zs * xs
    column = -(-length // piece // 128) * 128
    folded = jnp.pad(total, ((0, 0), (0, piece * column - length))).reshape(ys, piece, column)
    whole = jnp.broadcast_to(gathered, (ys,) + gathered.shape)
    arrived = exchanged(jnp.concatenate([whole, folded], axis=2), 2)
    gathered = arrived.reshape(ys * piece, length + column)
    total = jnp.sum(arrived[:, :, length:].astype(f32), axis=0).reshape(1, -1)[:, :length]

    other_weight = swapped_core(gathered[:, :length])
    place = position % half
    weight_row = 2 * lat_index(place // xs % zs, place % xs, place // piece, factors)
    weight_row = weight_row + (core ^ (position // half))
    weight_order = (weight_row[:, None] == jnp.arange(outs)[None, :]).astype(bf16)

    output = pl.pallas_call(
        lambda *refs: output_kernel(tile_count, *refs),
        out_shape=jax.ShapeDtypeStruct((rows, cols, outs), bf16),
        in_specs=vmem(4),
        out_specs=pl.BlockSpec(memory_space=pltpu.VMEM),
        cost_estimate=pl.CostEstimate(
            flops=2 * cells * outs * (length + outs), bytes_accessed=8 * cells * length, transcendentals=0
        ),
        name="mixing",
    )(features, gathered, other_weight, weight_order)

    scale = 1.0 / math.sqrt(rows * lax.axis_size("lat") * cols * lax.axis_size("lon"))
    lon_size = lax.axis_size("lon")
    spread = jnp.broadcast_to(total * scale, (lon_size,) + total.shape)
    arrived = lax.all_to_all(spread, "lon", 0, 0)
    arrived, output = lax.optimization_barrier((arrived, output))
    grad_weight = jnp.sum(arrived.reshape(lon_size // 2, 2, nbasis * channels), axis=0)
    return (output, grad_weight)


def solution(mesh):
    return jax.shard_map(
        shards,
        mesh=mesh,
        in_specs=(
            P("lat", "lon", None),
            P("lat", None, None, None),
            P("lat", None),
            P("lat", None),
            P("lat", "lon", None),
        ),
        out_specs=(P("lat", "lon", None), P("lat", None)),
        check_vma=False,
    )
```

```python
import math

import jax
import jax.numpy as jnp
from jax import lax
from jax.experimental import pallas as pl
from jax.experimental.pallas import tpu as pltpu
from jax.sharding import PartitionSpec as P

FACTORS = {128: (4, 4, 8), 16: (4, 1, 4)}
TILE = 8


def dot(a, b, contract):
    return lax.dot_general(a, b, (contract, ((), ())), preferred_element_type=jnp.float32)


def lat_index(z, x, y, factors):
    return (z * factors[1] + x) * factors[2] + y


def lat_coords(index, factors):
    return index // (factors[1] * factors[2]), index // factors[2] % factors[1], index % factors[2]


def groups(dims, factors):
    members = {}
    for index in range(factors[0] * factors[1] * factors[2]):
        coords = lat_coords(index, factors)
        fixed = tuple(coords[d] for d in range(3) if d not in dims)
        members.setdefault(fixed, []).append(index)
    return [members[fixed] for fixed in sorted(members)]


def swapped_core(block):
    return lax.ppermute(block, "lon", [(i, i ^ 1) for i in range(lax.axis_size("lon"))])


def passed_along(block, by):
    count = lax.axis_size("lat")
    return lax.ppermute(block, "lat", [(i, i + by) for i in range(count) if 0 <= i + by < count])


def paired(block, axis, first, loop):
    count = lax.axis_size(axis)
    pairs = []
    for low in range(first, count, 2):
        high = low + 1
        if high == count:
            if not loop:
                continue
            high = 0
        pairs += [(low, high), (high, low)]
    return lax.ppermute(block, axis, pairs)


def spread_over(block, dim, factors):
    copies = jnp.broadcast_to(block, (factors[dim],) + block.shape)
    joined = lax.all_to_all(copies, "lat", 0, 0, axis_index_groups=groups((dim,), factors))
    return joined.reshape(-1, block.shape[1])


def doubled(block, mask, after, factors):
    mask = mask * factors[1] * factors[2]
    pairs = [(i, i ^ mask) for i in range(lax.axis_size("lat"))]
    other = lax.ppermute(block, "lat", pairs)
    block, after = lax.optimization_barrier((block, after))
    return jnp.concatenate([block, other], axis=0), after


def band_kernel(rows_ref, band_ref):
    count, width = rows_ref.shape
    for start in range(0, count, 2):
        pair = []
        for row in (start, start + 1):
            spread = jnp.broadcast_to(rows_ref[row : row + 1, :], (TILE, width))
            pair.append(pltpu.roll(spread, 0, 1, stride=1, stride_axis=0))
        both = jnp.concatenate(pair, axis=0).astype(jnp.bfloat16)
        band_ref[start * TILE : (start + 2) * TILE, :] = both


def feature_kernel(nbasis, tile_count, *refs):
    band_ref, cot_ref = refs[0], refs[1]
    window_refs = refs[2:9]
    features_ref, keep_ref, send_ref = refs[9:]
    rows = window_refs[0].shape[0]
    reach = band_ref.shape[1] // (7 * rows)
    per_tile = rows * TILE
    band = band_ref[...]
    for tile in range(tile_count):
        pieces = []
        for ref in window_refs:
            for row in range(rows):
                pieces.append(ref[row, tile * TILE : tile * TILE + reach, :])
        window = jnp.concatenate(pieces, axis=0)
        summed = dot(band, window, ((1,), (0,))).astype(jnp.bfloat16)
        for k in range(nbasis):
            features_ref[k, tile * per_tile : (tile + 1) * per_tile, :] = summed[
                k * per_tile : (k + 1) * per_tile
            ]
    half = cot_ref.shape[0] // 2
    channels = features_ref.shape[2]
    for k in range(nbasis):
        term = dot(cot_ref[...], features_ref[k], ((1,), (0,)))
        span = slice(k * channels, (k + 1) * channels)
        keep_ref[:, span] = term[:half].astype(keep_ref.dtype)
        send_ref[:, span] = term[half:].astype(send_ref.dtype)


def output_kernel(tile_count, features_ref, mine_ref, other_ref, order_ref, output_ref):
    nbasis, cells, channels = features_ref.shape
    rows = output_ref.shape[0]
    total = jnp.zeros((cells, order_ref.shape[0]), jnp.float32)
    for k in range(nbasis):
        span = slice(k * channels, (k + 1) * channels)
        piece = jnp.concatenate([mine_ref[:, span], other_ref[:, span]], axis=0)
        total = total + dot(features_ref[k], piece, ((1,), (1,)))
    mixed = dot(total.astype(jnp.bfloat16), order_ref[...], ((1,), (0,))).astype(jnp.bfloat16)
    for tile in range(tile_count):
        for row in range(rows):
            start = (tile * rows + row) * TILE
            output_ref[row, tile * TILE : (tile + 1) * TILE, :] = mixed[start : start + TILE]


def vmem(count):
    return [pl.BlockSpec(memory_space=pltpu.VMEM)] * count


def shards(fields, basis, spans, weight, cotangent):
    rows, cols, channels = fields.shape
    extent, nbasis, width = basis.shape[1:]
    outs = cotangent.shape[2]
    reach = (width - 1) // 2
    factors = FACTORS[lax.axis_size("lat")]
    lat = lax.axis_index("lat")
    lon = lax.axis_index("lon")
    core = lon % 2
    tile_count = cols // TILE
    window_rows = extent + rows - 1
    window_cols = TILE + width - 1
    cells = rows * cols
    bf16 = jnp.bfloat16

    offsets = jnp.arange(width) - reach
    validity = jnp.abs(offsets)[None, None, :] <= spans[:, :, None]
    masked = jnp.where(validity[:, :, None, :], basis, jnp.zeros_like(basis))
    masked = jnp.transpose(masked, (2, 0, 1, 3)).astype(jnp.float32)
    band_rows = jnp.stack(
        [
            jnp.pad(masked[:, row], ((0, 0), (row, rows - 1 - row), (0, window_cols - width)))
            for row in range(rows)
        ],
        axis=1,
    ).reshape(nbasis * rows, window_rows * window_cols)
    band = pl.pallas_call(
        band_kernel,
        out_shape=jax.ShapeDtypeStruct((nbasis * rows * TILE, window_rows * window_cols), bf16),
        in_specs=vmem(1),
        out_specs=pl.BlockSpec(memory_space=pltpu.VMEM),
    )(band_rows)

    zs, xs, ys = factors
    position = jnp.arange(outs)
    half = outs // 2
    away = (
        2
        * lat_index(
            position // ys % zs, position // (ys * zs) % xs, position % ys, factors
        )
        + (core ^ (position // half))
    )
    cot_order = (away[:, None] == jnp.arange(outs)[None, :]).astype(bf16)
    cot_cells = jnp.transpose(cotangent.reshape(rows, tile_count, TILE, outs), (1, 0, 2, 3))
    cot = dot(cot_order, cot_cells.reshape(cells, outs), ((1,), (1,))).astype(bf16)

    low, high = fields[:, :reach], fields[:, cols - reach :]
    near_edge = paired(jnp.where(core == 0, high, low), "lon", 0, True)
    far_edge = paired(jnp.where(core == 0, low, high), "lon", 1, True)
    left = jnp.where(core == 0, far_edge, near_edge)
    right = jnp.where(core == 0, near_edge, far_edge)
    own = jnp.concatenate([left, fields, right], axis=1)
    windows = {0: own}
    for by in (3, -3, 2, -2, 1, -1):
        windows[by] = passed_along(own, by)

    mine = lax.dynamic_slice_in_dim(weight, core, 1, 0)
    windows[3], mine = lax.optimization_barrier((windows[3], mine))
    gathered = spread_over(mine, 2, factors)
    windows[-1], gathered, band, cot = lax.optimization_barrier((windows[-1], gathered, band, cot))
    pieces = [windows[by] for by in (3, 2, 1, 0, -1, -2, -3)]

    features, keep, send = pl.pallas_call(
        lambda *refs: feature_kernel(nbasis, tile_count, *refs),
        out_shape=(
            jax.ShapeDtypeStruct((nbasis, cells, channels), bf16),
            jax.ShapeDtypeStruct((half, nbasis * channels), bf16),
            jax.ShapeDtypeStruct((half, nbasis * channels), bf16),
        ),
        in_specs=vmem(9),
        out_specs=tuple(vmem(3)),
        name="features",
    )(band, cot, *pieces)

    f32 = jnp.float32
    length = nbasis * channels

    def exchanged(block, dim):
        block = block.reshape(factors[dim], -1, block.shape[-1])
        return lax.all_to_all(block, "lat", 0, 0, axis_index_groups=groups((dim,), factors))

    total = (keep.astype(f32) + swapped_core(send).astype(f32)).astype(bf16)
    total = total.reshape(xs, zs * ys, length)
    third = length // 3
    folded = jnp.concatenate([gathered[:, n * third : (n + 1) * third] for n in range(3)], axis=0)
    folded = jnp.pad(folded, ((0, total.shape[1] - 3 * ys), (0, 0)))
    folded = jnp.broadcast_to(folded, (xs,) + folded.shape)
    arrived = exchanged(jnp.concatenate([total, folded], axis=2), 1)
    total = jnp.sum(arrived[:, :, :length].astype(f32), axis=0).astype(bf16)
    gathered = jnp.concatenate(
        [arrived[:, n * ys : (n + 1) * ys, length:] for n in range(3)], axis=2
    ).reshape(xs * ys, length)

    total = jnp.sum(exchanged(total, 0).astype(f32), axis=0)
    gathered, total = doubled(gathered, 1, total, factors)
    total = jnp.sum(exchanged(total, 2), axis=0)
    scale = 1.0 / math.sqrt(rows * lax.axis_size("lat") * cols * lax.axis_size("lon"))
    lon_size = lax.axis_size("lon")
    spread = jnp.broadcast_to(total * scale, (lon_size,) + total.shape)
    if zs == 4:
        gathered, spread = doubled(gathered, 2, spread, factors)
    other_weight = swapped_core(gathered)
    place = position % half
    from_z = (lat // (xs * ys)) ^ (place // (xs * ys))
    weight_row = 2 * lat_index(from_z, place // ys % xs, place % ys, factors)
    weight_row = weight_row + (core ^ (position // half))
    weight_order = (weight_row[:, None] == jnp.arange(outs)[None, :]).astype(bf16)

    output = pl.pallas_call(
        lambda *refs: output_kernel(tile_count, *refs),
        out_shape=jax.ShapeDtypeStruct((rows, cols, outs), bf16),
        in_specs=vmem(4),
        out_specs=pl.BlockSpec(memory_space=pltpu.VMEM),
        cost_estimate=pl.CostEstimate(
            flops=2 * cells * outs * (length + outs), bytes_accessed=8 * cells * length, transcendentals=0
        ),
        name="mixing",
    )(features, gathered, other_weight, weight_order)

    arrived = lax.all_to_all(spread, "lon", 0, 0)
    arrived, output = lax.optimization_barrier((arrived, output))
    grad_weight = jnp.sum(arrived.reshape(lon_size // 2, 2, nbasis * channels), axis=0)
    return (output, grad_weight)


def solution(mesh):
    return jax.shard_map(
        shards,
        mesh=mesh,
        in_specs=(
            P("lat", "lon", None),
            P("lat", None, None, None),
            P("lat", None),
            P("lat", None),
            P("lat", "lon", None),
        ),
        out_specs=(P("lat", "lon", None), P("lat", None)),
        check_vma=False,
    )
```

```python
import math

import jax
import jax.numpy as jnp
from jax import lax
from jax.experimental import pallas as pl
from jax.experimental.pallas import tpu as pltpu
from jax.sharding import PartitionSpec as P

FACTORS = {128: (4, 4, 8), 16: (4, 1, 4)}
TILE = 8


def dot(a, b, contract):
    return lax.dot_general(a, b, (contract, ((), ())), preferred_element_type=jnp.float32)


def lat_index(z, x, y, factors):
    return (z * factors[1] + x) * factors[2] + y


def lat_coords(index, factors):
    return index // (factors[1] * factors[2]), index // factors[2] % factors[1], index % factors[2]


def groups(dims, factors):
    members = {}
    for index in range(factors[0] * factors[1] * factors[2]):
        coords = lat_coords(index, factors)
        fixed = tuple(coords[d] for d in range(3) if d not in dims)
        members.setdefault(fixed, []).append(index)
    return [members[fixed] for fixed in sorted(members)]


def swapped_core(block):
    return lax.ppermute(block, "lon", [(i, i ^ 1) for i in range(lax.axis_size("lon"))])


def passed_along(block, by):
    count = lax.axis_size("lat")
    return lax.ppermute(block, "lat", [(i, i + by) for i in range(count) if 0 <= i + by < count])


def paired(block, axis, first, loop):
    count = lax.axis_size(axis)
    pairs = []
    for low in range(first, count, 2):
        high = low + 1
        if high == count:
            if not loop:
                continue
            high = 0
        pairs += [(low, high), (high, low)]
    return lax.ppermute(block, axis, pairs)


def spread_over(block, dims, factors):
    members = groups(dims, factors)
    copies = jnp.broadcast_to(block, (len(members[0]),) + block.shape)
    joined = lax.all_to_all(copies, "lat", 0, 0, axis_index_groups=members)
    return joined.reshape(-1, block.shape[1])


def doubled(block, mask, factors):
    mask = mask * factors[1] * factors[2]
    pairs = [(i, i ^ mask) for i in range(lax.axis_size("lat"))]
    return jnp.concatenate([block, lax.ppermute(block, "lat", pairs)], axis=0)


def band_kernel(rows_ref, band_ref):
    count, width = rows_ref.shape
    for start in range(0, count, 2):
        pair = []
        for row in (start, start + 1):
            spread = jnp.broadcast_to(rows_ref[row : row + 1, :], (TILE, width))
            pair.append(pltpu.roll(spread, 0, 1, stride=1, stride_axis=0))
        both = jnp.concatenate(pair, axis=0).astype(jnp.bfloat16)
        band_ref[start * TILE : (start + 2) * TILE, :] = both


def feature_kernel(nbasis, tile_count, *refs):
    band_ref, cot_ref = refs[0], refs[1]
    window_refs = refs[2:9]
    features_ref, keep_ref, send_ref = refs[9:]
    rows = window_refs[0].shape[0]
    reach = band_ref.shape[1] // (7 * rows)
    per_tile = rows * TILE
    band = band_ref[...]
    for tile in range(tile_count):
        pieces = []
        for ref in window_refs:
            for row in range(rows):
                pieces.append(ref[row, tile * TILE : tile * TILE + reach, :])
        window = jnp.concatenate(pieces, axis=0)
        summed = dot(band, window, ((1,), (0,))).astype(jnp.bfloat16)
        for k in range(nbasis):
            features_ref[k, tile * per_tile : (tile + 1) * per_tile, :] = summed[
                k * per_tile : (k + 1) * per_tile
            ]
    half = cot_ref.shape[0] // 2
    channels = features_ref.shape[2]
    for k in range(nbasis):
        term = dot(cot_ref[...], features_ref[k], ((1,), (0,)))
        span = slice(k * channels, (k + 1) * channels)
        keep_ref[:, span] = term[:half].astype(keep_ref.dtype)
        send_ref[:, span] = term[half:].astype(send_ref.dtype)


def output_kernel(tile_count, features_ref, mine_ref, other_ref, order_ref, output_ref):
    nbasis, cells, channels = features_ref.shape
    rows = output_ref.shape[0]
    total = jnp.zeros((cells, order_ref.shape[0]), jnp.float32)
    for k in range(nbasis):
        span = slice(k * channels, (k + 1) * channels)
        piece = jnp.concatenate([mine_ref[:, span], other_ref[:, span]], axis=0)
        total = total + dot(features_ref[k], piece, ((1,), (1,)))
    mixed = dot(total.astype(jnp.bfloat16), order_ref[...], ((1,), (0,))).astype(jnp.bfloat16)
    for tile in range(tile_count):
        for row in range(rows):
            start = (tile * rows + row) * TILE
            output_ref[row, tile * TILE : (tile + 1) * TILE, :] = mixed[start : start + TILE]


def vmem(count):
    return [pl.BlockSpec(memory_space=pltpu.VMEM)] * count


def shards(fields, basis, spans, weight, cotangent):
    rows, cols, channels = fields.shape
    extent, nbasis, width = basis.shape[1:]
    outs = cotangent.shape[2]
    reach = (width - 1) // 2
    factors = FACTORS[lax.axis_size("lat")]
    lat = lax.axis_index("lat")
    lon = lax.axis_index("lon")
    core = lon % 2
    tile_count = cols // TILE
    window_rows = extent + rows - 1
    window_cols = TILE + width - 1
    cells = rows * cols
    bf16 = jnp.bfloat16

    offsets = jnp.arange(width) - reach
    validity = jnp.abs(offsets)[None, None, :] <= spans[:, :, None]
    masked = jnp.where(validity[:, :, None, :], basis, jnp.zeros_like(basis))
    masked = jnp.transpose(masked, (2, 0, 1, 3)).astype(jnp.float32)
    band_rows = jnp.stack(
        [
            jnp.pad(masked[:, row], ((0, 0), (row, rows - 1 - row), (0, window_cols - width)))
            for row in range(rows)
        ],
        axis=1,
    ).reshape(nbasis * rows, window_rows * window_cols)
    band = pl.pallas_call(
        band_kernel,
        out_shape=jax.ShapeDtypeStruct((nbasis * rows * TILE, window_rows * window_cols), bf16),
        in_specs=vmem(1),
        out_specs=pl.BlockSpec(memory_space=pltpu.VMEM),
    )(band_rows)

    zs, xs, ys = factors
    position = jnp.arange(outs)
    half = outs // 2
    away = (
        2
        * lat_index(
            position // ys % zs, position // (ys * zs) % xs, position % ys, factors
        )
        + (core ^ (position // half))
    )
    cot_order = (away[:, None] == jnp.arange(outs)[None, :]).astype(bf16)
    cot_cells = jnp.transpose(cotangent.reshape(rows, tile_count, TILE, outs), (1, 0, 2, 3))
    cot = dot(cot_order, cot_cells.reshape(cells, outs), ((1,), (1,))).astype(bf16)

    low, high = fields[:, :reach], fields[:, cols - reach :]
    near_edge = paired(jnp.where(core == 0, high, low), "lon", 0, True)
    far_edge = paired(jnp.where(core == 0, low, high), "lon", 1, True)
    left = jnp.where(core == 0, far_edge, near_edge)
    right = jnp.where(core == 0, near_edge, far_edge)
    own = jnp.concatenate([left, fields, right], axis=1)
    gathered = spread_over(lax.dynamic_slice_in_dim(weight, core, 1, 0), (1, 2), factors)
    own, gathered = lax.optimization_barrier((own, gathered))
    gathered = doubled(gathered, 1, factors)
    windows = {0: own}
    for by in (3, -3, 2, -2, 1, -1):
        windows[by] = passed_along(own, by)
    windows[-1], band, cot, gathered = lax.optimization_barrier((windows[-1], band, cot, gathered))
    pieces = [windows[by] for by in (3, 2, 1, 0, -1, -2, -3)]

    features, keep, send = pl.pallas_call(
        lambda *refs: feature_kernel(nbasis, tile_count, *refs),
        out_shape=(
            jax.ShapeDtypeStruct((nbasis, cells, channels), bf16),
            jax.ShapeDtypeStruct((half, nbasis * channels), bf16),
            jax.ShapeDtypeStruct((half, nbasis * channels), bf16),
        ),
        in_specs=vmem(9),
        out_specs=tuple(vmem(3)),
        name="features",
    )(band, cot, *pieces)

    f32 = jnp.float32
    length = nbasis * channels

    def exchanged(block, dim):
        block = block.reshape(factors[dim], -1, block.shape[-1])
        return lax.all_to_all(block, "lat", 0, 0, axis_index_groups=groups((dim,), factors))

    total = (keep.astype(f32) + swapped_core(send).astype(f32)).astype(bf16)
    total, gathered = lax.optimization_barrier((total, gathered))
    total = jnp.sum(exchanged(total, 1).astype(f32), axis=0).astype(bf16)
    if zs == 4:
        gathered = doubled(gathered, 2, factors)
    total, gathered = lax.optimization_barrier((total, gathered))
    total = jnp.sum(exchanged(total, 0).astype(f32), axis=0)
    other_weight = swapped_core(gathered)
    total = jnp.sum(exchanged(total, 2), axis=0)
    scale = 1.0 / math.sqrt(rows * lax.axis_size("lat") * cols * lax.axis_size("lon"))
    lon_size = lax.axis_size("lon")
    spread = jnp.broadcast_to(total * scale, (lon_size,) + total.shape)
    place = position % half
    from_z = (lat // (xs * ys)) ^ (place // (xs * ys))
    weight_row = 2 * lat_index(from_z, place // ys % xs, place % ys, factors)
    weight_row = weight_row + (core ^ (position // half))
    weight_order = (weight_row[:, None] == jnp.arange(outs)[None, :]).astype(bf16)

    output = pl.pallas_call(
        lambda *refs: output_kernel(tile_count, *refs),
        out_shape=jax.ShapeDtypeStruct((rows, cols, outs), bf16),
        in_specs=vmem(4),
        out_specs=pl.BlockSpec(memory_space=pltpu.VMEM),
        cost_estimate=pl.CostEstimate(
            flops=2 * cells * outs * (length + outs), bytes_accessed=8 * cells * length, transcendentals=0
        ),
        name="mixing",
    )(features, gathered, other_weight, weight_order)

    arrived = lax.all_to_all(spread, "lon", 0, 0)
    arrived, output = lax.optimization_barrier((arrived, output))
    grad_weight = jnp.sum(arrived.reshape(lon_size // 2, 2, nbasis * channels), axis=0)
    return (output, grad_weight)


def solution(mesh):
    return jax.shard_map(
        shards,
        mesh=mesh,
        in_specs=(
            P("lat", "lon", None),
            P("lat", None, None, None),
            P("lat", None),
            P("lat", None),
            P("lat", "lon", None),
        ),
        out_specs=(P("lat", "lon", None), P("lat", None)),
        check_vma=False,
    )
```

```python
import math

import jax
import jax.numpy as jnp
from jax import lax
from jax.experimental import pallas as pl
from jax.experimental.pallas import tpu as pltpu
from jax.sharding import PartitionSpec as P

FACTORS = {128: (4, 4, 8), 16: (4, 1, 4)}
TILE = 8


def dot(a, b, contract):
    return lax.dot_general(a, b, (contract, ((), ())), preferred_element_type=jnp.float32)


def lat_index(z, x, y, factors):
    return (z * factors[1] + x) * factors[2] + y


def lat_coords(index, factors):
    return index // (factors[1] * factors[2]), index // factors[2] % factors[1], index % factors[2]


def groups(dims, factors):
    members = {}
    for index in range(factors[0] * factors[1] * factors[2]):
        coords = lat_coords(index, factors)
        fixed = tuple(coords[d] for d in range(3) if d not in dims)
        members.setdefault(fixed, []).append(index)
    return [members[fixed] for fixed in sorted(members)]


def swapped_core(block):
    return lax.ppermute(block, "lon", [(i, i ^ 1) for i in range(lax.axis_size("lon"))])


def passed_along(block, by):
    count = lax.axis_size("lat")
    return lax.ppermute(block, "lat", [(i, i + by) for i in range(count) if 0 <= i + by < count])


def paired(block, axis, first, loop):
    count = lax.axis_size(axis)
    pairs = []
    for low in range(first, count, 2):
        high = low + 1
        if high == count:
            if not loop:
                continue
            high = 0
        pairs += [(low, high), (high, low)]
    return lax.ppermute(block, axis, pairs)


def band_kernel(rows_ref, band_ref):
    count, width = rows_ref.shape
    for start in range(0, count, 2):
        pair = []
        for row in (start, start + 1):
            spread = jnp.broadcast_to(rows_ref[row : row + 1, :], (TILE, width))
            pair.append(pltpu.roll(spread, 0, 1, stride=1, stride_axis=0))
        both = jnp.concatenate(pair, axis=0).astype(jnp.bfloat16)
        band_ref[start * TILE : (start + 2) * TILE, :] = both


def feature_kernel(nbasis, tile_count, *refs):
    band_ref, cot_ref = refs[0], refs[1]
    window_refs = refs[2:9]
    features_ref, keep_ref, send_ref = refs[9:]
    rows = window_refs[0].shape[0]
    reach = band_ref.shape[1] // (7 * rows)
    per_tile = rows * TILE
    band = band_ref[...]
    for tile in range(tile_count):
        pieces = []
        for ref in window_refs:
            for row in range(rows):
                pieces.append(ref[row, tile * TILE : tile * TILE + reach, :])
        window = jnp.concatenate(pieces, axis=0)
        summed = dot(band, window, ((1,), (0,))).astype(jnp.bfloat16)
        for k in range(nbasis):
            features_ref[k, tile * per_tile : (tile + 1) * per_tile, :] = summed[
                k * per_tile : (k + 1) * per_tile
            ]
    half = cot_ref.shape[0] // 2
    channels = features_ref.shape[2]
    for k in range(nbasis):
        term = dot(cot_ref[...], features_ref[k], ((1,), (0,)))
        span = slice(k * channels, (k + 1) * channels)
        keep_ref[:, span] = term[:half].astype(keep_ref.dtype)
        send_ref[:, span] = term[half:].astype(send_ref.dtype)


def output_kernel(tile_count, features_ref, mine_ref, other_ref, order_ref, output_ref):
    nbasis, cells, channels = features_ref.shape
    rows = output_ref.shape[0]
    total = jnp.zeros((cells, order_ref.shape[0]), jnp.float32)
    for k in range(nbasis):
        span = slice(k * channels, (k + 1) * channels)
        piece = jnp.concatenate([mine_ref[:, span], other_ref[:, span]], axis=0)
        total = total + dot(features_ref[k], piece, ((1,), (1,)))
    mixed = dot(total.astype(jnp.bfloat16), order_ref[...], ((1,), (0,))).astype(jnp.bfloat16)
    for tile in range(tile_count):
        for row in range(rows):
            start = (tile * rows + row) * TILE
            output_ref[row, tile * TILE : (tile + 1) * TILE, :] = mixed[start : start + TILE]


def vmem(count):
    return [pl.BlockSpec(memory_space=pltpu.VMEM)] * count


def shards(fields, basis, spans, weight, cotangent):
    rows, cols, channels = fields.shape
    extent, nbasis, width = basis.shape[1:]
    outs = cotangent.shape[2]
    reach = (width - 1) // 2
    factors = FACTORS[lax.axis_size("lat")]
    lat = lax.axis_index("lat")
    lon = lax.axis_index("lon")
    core = lon % 2
    tile_count = cols // TILE
    window_rows = extent + rows - 1
    window_cols = TILE + width - 1
    cells = rows * cols
    bf16 = jnp.bfloat16

    offsets = jnp.arange(width) - reach
    validity = jnp.abs(offsets)[None, None, :] <= spans[:, :, None]
    masked = jnp.where(validity[:, :, None, :], basis, jnp.zeros_like(basis))
    masked = jnp.transpose(masked, (2, 0, 1, 3)).astype(jnp.float32)
    band_rows = jnp.stack(
        [
            jnp.pad(masked[:, row], ((0, 0), (row, rows - 1 - row), (0, window_cols - width)))
            for row in range(rows)
        ],
        axis=1,
    ).reshape(nbasis * rows, window_rows * window_cols)
    band = pl.pallas_call(
        band_kernel,
        out_shape=jax.ShapeDtypeStruct((nbasis * rows * TILE, window_rows * window_cols), bf16),
        in_specs=vmem(1),
        out_specs=pl.BlockSpec(memory_space=pltpu.VMEM),
    )(band_rows)

    zs, xs, ys = factors
    position = jnp.arange(outs)
    half = outs // 2
    away = (
        2
        * lat_index(
            position // ys % zs, position // (ys * zs) % xs, position % ys, factors
        )
        + (core ^ (position // half))
    )
    cot_order = (away[:, None] == jnp.arange(outs)[None, :]).astype(bf16)
    cot_cells = jnp.transpose(cotangent.reshape(rows, tile_count, TILE, outs), (1, 0, 2, 3))
    cot = dot(cot_order, cot_cells.reshape(cells, outs), ((1,), (1,))).astype(bf16)

    low, high = fields[:, :reach], fields[:, cols - reach :]
    near_edge = paired(jnp.where(core == 0, high, low), "lon", 0, True)
    far_edge = paired(jnp.where(core == 0, low, high), "lon", 1, True)
    left = jnp.where(core == 0, far_edge, near_edge)
    right = jnp.where(core == 0, near_edge, far_edge)
    own = jnp.concatenate([left, fields, right], axis=1)
    windows = {0: own}
    for by in (3, -3, 2, -2, 1, -1):
        windows[by] = passed_along(own, by)

    windows[-1], band, cot = lax.optimization_barrier((windows[-1], band, cot))
    pieces = [windows[by] for by in (3, 2, 1, 0, -1, -2, -3)]

    features, keep, send = pl.pallas_call(
        lambda *refs: feature_kernel(nbasis, tile_count, *refs),
        out_shape=(
            jax.ShapeDtypeStruct((nbasis, cells, channels), bf16),
            jax.ShapeDtypeStruct((half, nbasis * channels), bf16),
            jax.ShapeDtypeStruct((half, nbasis * channels), bf16),
        ),
        in_specs=vmem(9),
        out_specs=tuple(vmem(3)),
        name="features",
    )(band, cot, *pieces)

    f32 = jnp.float32
    length = nbasis * channels

    def exchanged(block, dim):
        block = block.reshape(factors[dim], -1, block.shape[-1])
        return lax.all_to_all(block, "lat", 0, 0, axis_index_groups=groups((dim,), factors))

    total = (keep.astype(f32) + swapped_core(send).astype(f32)).astype(bf16)
    count = zs * ys
    column = -(-length // count // 128) * 128
    mine = lax.dynamic_slice_in_dim(weight, core, 1, 0)
    folded = jnp.pad(mine, ((0, 0), (0, count * column - length))).reshape(1, count, column)
    folded = jnp.broadcast_to(folded, (xs, count, column))
    total = total.reshape(xs, count, length)
    arrived = exchanged(jnp.concatenate([total, folded], axis=2), 1)
    total = jnp.sum(arrived[:, :, :length].astype(f32), axis=0).astype(bf16)
    gathered = arrived[:, :, length:].reshape(xs, count * column)[:, :length]

    total = total.reshape(zs, ys, length)
    folded = jnp.concatenate([gathered[:, : length // 2], gathered[:, length // 2 :]], axis=0)
    folded = jnp.pad(folded, ((0, ys - folded.shape[0]), (0, 0)))
    folded = jnp.broadcast_to(folded, (zs,) + folded.shape)
    arrived = exchanged(jnp.concatenate([total, folded], axis=2), 0)
    total = jnp.sum(arrived[:, :, :length].astype(f32), axis=0).astype(bf16)
    gathered = jnp.concatenate(
        [arrived[:, :xs, length:], arrived[:, xs : 2 * xs, length:]], axis=2
    ).reshape(zs * xs, length)

    piece = zs * xs
    column = -(-length // piece // 128) * 128
    folded = jnp.pad(total, ((0, 0), (0, piece * column - length))).reshape(ys, piece, column)
    whole = jnp.broadcast_to(gathered, (ys,) + gathered.shape)
    arrived = exchanged(jnp.concatenate([whole, folded], axis=2), 2)
    gathered = arrived.reshape(ys * piece, length + column)
    total = jnp.sum(arrived[:, :, length:].astype(f32), axis=0).reshape(1, -1)[:, :length]

    other_weight = swapped_core(gathered[:, :length])
    place = position % half
    weight_row = 2 * lat_index(place // xs % zs, place % xs, place // piece, factors)
    weight_row = weight_row + (core ^ (position // half))
    weight_order = (weight_row[:, None] == jnp.arange(outs)[None, :]).astype(bf16)

    output = pl.pallas_call(
        lambda *refs: output_kernel(tile_count, *refs),
        out_shape=jax.ShapeDtypeStruct((rows, cols, outs), bf16),
        in_specs=vmem(4),
        out_specs=pl.BlockSpec(memory_space=pltpu.VMEM),
        cost_estimate=pl.CostEstimate(
            flops=2 * cells * outs * (length + outs), bytes_accessed=8 * cells * length, transcendentals=0
        ),
        name="mixing",
    )(features, gathered, other_weight, weight_order)

    scale = 1.0 / math.sqrt(rows * lax.axis_size("lat") * cols * lax.axis_size("lon"))
    lon_size = lax.axis_size("lon")
    spread = jnp.broadcast_to(total * scale, (lon_size,) + total.shape)
    arrived = lax.all_to_all(spread, "lon", 0, 0)
    arrived, output = lax.optimization_barrier((arrived, output))
    grad_weight = jnp.sum(arrived.reshape(lon_size // 2, 2, nbasis * channels), axis=0)
    return (output, grad_weight)


def solution(mesh):
    return jax.shard_map(
        shards,
        mesh=mesh,
        in_specs=(
            P("lat", "lon", None),
            P("lat", None, None, None),
            P("lat", None),
            P("lat", None),
            P("lat", "lon", None),
        ),
        out_specs=(P("lat", "lon", None), P("lat", None)),
        check_vma=False,
    )
```

```python
import math

import jax
import jax.numpy as jnp
from jax import lax
from jax.experimental import pallas as pl
from jax.experimental.pallas import tpu as pltpu
from jax.sharding import PartitionSpec as P

FACTORS = {128: (4, 4, 8), 16: (4, 1, 4)}
TILE = 8


def dot(a, b, contract):
    return lax.dot_general(a, b, (contract, ((), ())), preferred_element_type=jnp.float32)


def lat_index(z, x, y, factors):
    return (z * factors[1] + x) * factors[2] + y


def lat_coords(index, factors):
    return index // (factors[1] * factors[2]), index // factors[2] % factors[1], index % factors[2]


def groups(dims, factors):
    members = {}
    for index in range(factors[0] * factors[1] * factors[2]):
        coords = lat_coords(index, factors)
        fixed = tuple(coords[d] for d in range(3) if d not in dims)
        members.setdefault(fixed, []).append(index)
    return [members[fixed] for fixed in sorted(members)]


def swapped_core(block):
    return lax.ppermute(block, "lon", [(i, i ^ 1) for i in range(lax.axis_size("lon"))])


def paired(block, axis, first, loop):
    count = lax.axis_size(axis)
    pairs = []
    for low in range(first, count, 2):
        high = low + 1
        if high == count:
            if not loop:
                continue
            high = 0
        pairs += [(low, high), (high, low)]
    return lax.ppermute(block, axis, pairs)


def band_kernel(rows_ref, band_ref):
    count, width = rows_ref.shape
    for start in range(0, count, 2):
        pair = []
        for row in (start, start + 1):
            spread = jnp.broadcast_to(rows_ref[row : row + 1, :], (TILE, width))
            pair.append(pltpu.roll(spread, 0, 1, stride=1, stride_axis=0))
        both = jnp.concatenate(pair, axis=0).astype(jnp.bfloat16)
        band_ref[start * TILE : (start + 2) * TILE, :] = both


def feature_kernel(nbasis, tile_count, *refs):
    band_ref, cot_ref = refs[0], refs[1]
    window_refs = refs[2:9]
    features_ref, keep_ref, send_ref = refs[9:]
    rows = window_refs[0].shape[0]
    reach = band_ref.shape[1] // (7 * rows)
    per_tile = rows * TILE
    band = band_ref[...]
    for tile in range(tile_count):
        pieces = []
        for ref in window_refs:
            for row in range(rows):
                pieces.append(ref[row, tile * TILE : tile * TILE + reach, :])
        window = jnp.concatenate(pieces, axis=0)
        summed = dot(band, window, ((1,), (0,))).astype(jnp.bfloat16)
        for k in range(nbasis):
            features_ref[k, tile * per_tile : (tile + 1) * per_tile, :] = summed[
                k * per_tile : (k + 1) * per_tile
            ]
    half = cot_ref.shape[0] // 2
    channels = features_ref.shape[2]
    for k in range(nbasis):
        term = dot(cot_ref[...], features_ref[k], ((1,), (0,)))
        span = slice(k * channels, (k + 1) * channels)
        keep_ref[:, span] = term[:half].astype(keep_ref.dtype)
        send_ref[:, span] = term[half:].astype(send_ref.dtype)


def output_kernel(tile_count, features_ref, mine_ref, other_ref, order_ref, output_ref):
    nbasis, cells, channels = features_ref.shape
    rows = output_ref.shape[0]
    total = jnp.zeros((cells, order_ref.shape[0]), jnp.float32)
    for k in range(nbasis):
        span = slice(k * channels, (k + 1) * channels)
        piece = jnp.concatenate([mine_ref[:, span], other_ref[:, span]], axis=0)
        total = total + dot(features_ref[k], piece, ((1,), (1,)))
    mixed = dot(total.astype(jnp.bfloat16), order_ref[...], ((1,), (0,))).astype(jnp.bfloat16)
    for tile in range(tile_count):
        for row in range(rows):
            start = (tile * rows + row) * TILE
            output_ref[row, tile * TILE : (tile + 1) * TILE, :] = mixed[start : start + TILE]


def vmem(count):
    return [pl.BlockSpec(memory_space=pltpu.VMEM)] * count


def shards(fields, basis, spans, weight, cotangent):
    rows, cols, channels = fields.shape
    extent, nbasis, width = basis.shape[1:]
    outs = cotangent.shape[2]
    reach = (width - 1) // 2
    factors = FACTORS[lax.axis_size("lat")]
    lat = lax.axis_index("lat")
    lon = lax.axis_index("lon")
    core = lon % 2
    tile_count = cols // TILE
    window_rows = extent + rows - 1
    window_cols = TILE + width - 1
    cells = rows * cols
    bf16 = jnp.bfloat16

    offsets = jnp.arange(width) - reach
    validity = jnp.abs(offsets)[None, None, :] <= spans[:, :, None]
    masked = jnp.where(validity[:, :, None, :], basis, jnp.zeros_like(basis))
    masked = jnp.transpose(masked, (2, 0, 1, 3)).astype(jnp.float32)
    band_rows = jnp.stack(
        [
            jnp.pad(masked[:, row], ((0, 0), (row, rows - 1 - row), (0, window_cols - width)))
            for row in range(rows)
        ],
        axis=1,
    ).reshape(nbasis * rows, window_rows // rows, rows * window_cols)
    band_rows = jnp.where(lat % 2 == 0, band_rows[:, ::-1], band_rows)
    band_rows = band_rows.reshape(nbasis * rows, window_rows * window_cols)
    band = pl.pallas_call(
        band_kernel,
        out_shape=jax.ShapeDtypeStruct((nbasis * rows * TILE, window_rows * window_cols), bf16),
        in_specs=vmem(1),
        out_specs=pl.BlockSpec(memory_space=pltpu.VMEM),
    )(band_rows)

    zs, xs, ys = factors
    position = jnp.arange(outs)
    half = outs // 2
    away = (
        2
        * lat_index(
            position // ys % zs, position // (ys * zs) % xs, position % ys, factors
        )
        + (core ^ (position // half))
    )
    cot_order = (away[:, None] == jnp.arange(outs)[None, :]).astype(bf16)
    cot_cells = jnp.transpose(cotangent.reshape(rows, tile_count, TILE, outs), (1, 0, 2, 3))
    cot = dot(cot_order, cot_cells.reshape(cells, outs), ((1,), (1,))).astype(bf16)

    low, high = fields[:, :reach], fields[:, cols - reach :]
    near_edge = paired(jnp.where(core == 0, high, low), "lon", 0, True)
    far_edge = paired(jnp.where(core == 0, low, high), "lon", 1, True)
    left = jnp.where(core == 0, far_edge, near_edge)
    right = jnp.where(core == 0, near_edge, far_edge)
    own = jnp.concatenate([left, fields, right], axis=1)
    near, far = own, own
    nears, fars = [], []
    for turn in range(3):
        if turn == 2:
            near, band, cot = lax.optimization_barrier((near, band, cot))
        near, far = paired(far, "lat", 0, False), paired(near, "lat", 1, False)
        nears.append(near)
        fars.append(far)
    windows = nears[::-1] + [own] + fars

    features, keep, send = pl.pallas_call(
        lambda *refs: feature_kernel(nbasis, tile_count, *refs),
        out_shape=(
            jax.ShapeDtypeStruct((nbasis, cells, channels), bf16),
            jax.ShapeDtypeStruct((half, nbasis * channels), bf16),
            jax.ShapeDtypeStruct((half, nbasis * channels), bf16),
        ),
        in_specs=vmem(9),
        out_specs=tuple(vmem(3)),
        name="features",
    )(band, cot, *windows)

    f32 = jnp.float32
    length = nbasis * channels

    def exchanged(block, dim):
        block = block.reshape(factors[dim], -1, block.shape[-1])
        return lax.all_to_all(block, "lat", 0, 0, axis_index_groups=groups((dim,), factors))

    total = (keep.astype(f32) + swapped_core(send).astype(f32)).astype(bf16)
    count = zs * ys
    column = -(-length // count // 128) * 128
    mine = lax.dynamic_slice_in_dim(weight, core, 1, 0)
    folded = jnp.pad(mine, ((0, 0), (0, count * column - length))).reshape(1, count, column)
    folded = jnp.broadcast_to(folded, (xs, count, column))
    total = total.reshape(xs, count, length)
    arrived = exchanged(jnp.concatenate([total, folded], axis=2), 1)
    total = jnp.sum(arrived[:, :, :length].astype(f32), axis=0).astype(bf16)
    gathered = arrived[:, :, length:].reshape(xs, count * column)[:, :length]

    total = total.reshape(zs, ys, length)
    folded = jnp.concatenate([gathered[:, : length // 2], gathered[:, length // 2 :]], axis=0)
    folded = jnp.pad(folded, ((0, ys - folded.shape[0]), (0, 0)))
    folded = jnp.broadcast_to(folded, (zs,) + folded.shape)
    arrived = exchanged(jnp.concatenate([total, folded], axis=2), 0)
    total = jnp.sum(arrived[:, :, :length].astype(f32), axis=0).astype(bf16)
    gathered = jnp.concatenate(
        [arrived[:, :xs, length:], arrived[:, xs : 2 * xs, length:]], axis=2
    ).reshape(zs * xs, length)

    piece = zs * xs
    column = -(-length // piece // 128) * 128
    folded = jnp.pad(total, ((0, 0), (0, piece * column - length))).reshape(ys, piece, column)
    whole = jnp.broadcast_to(gathered, (ys,) + gathered.shape)
    arrived = exchanged(jnp.concatenate([whole, folded], axis=2), 2)
    gathered = arrived.reshape(ys * piece, length + column)
    total = jnp.sum(arrived[:, :, length:].astype(f32), axis=0).reshape(1, -1)[:, :length]

    other_weight = swapped_core(gathered[:, :length])
    place = position % half
    weight_row = 2 * lat_index(place // xs % zs, place % xs, place // piece, factors)
    weight_row = weight_row + (core ^ (position // half))
    weight_order = (weight_row[:, None] == jnp.arange(outs)[None, :]).astype(bf16)

    output = pl.pallas_call(
        lambda *refs: output_kernel(tile_count, *refs),
        out_shape=jax.ShapeDtypeStruct((rows, cols, outs), bf16),
        in_specs=vmem(4),
        out_specs=pl.BlockSpec(memory_space=pltpu.VMEM),
        cost_estimate=pl.CostEstimate(
            flops=2 * cells * outs * (length + outs), bytes_accessed=8 * cells * length, transcendentals=0
        ),
        name="mixing",
    )(features, gathered, other_weight, weight_order)

    scale = 1.0 / math.sqrt(rows * lax.axis_size("lat") * cols * lax.axis_size("lon"))
    lon_size = lax.axis_size("lon")
    spread = jnp.broadcast_to(total * scale, (lon_size,) + total.shape)
    arrived = lax.all_to_all(spread, "lon", 0, 0)
    arrived, output = lax.optimization_barrier((arrived, output))
    grad_weight = jnp.sum(arrived.reshape(lon_size // 2, 2, nbasis * channels), axis=0)
    return (output, grad_weight)


def solution(mesh):
    return jax.shard_map(
        shards,
        mesh=mesh,
        in_specs=(
            P("lat", "lon", None),
            P("lat", None, None, None),
            P("lat", None),
            P("lat", None),
            P("lat", "lon", None),
        ),
        out_specs=(P("lat", "lon", None), P("lat", None)),
        check_vma=False,
    )
```

```python
import math

import jax
import jax.numpy as jnp
from jax import lax
from jax.experimental import pallas as pl
from jax.experimental.pallas import tpu as pltpu
from jax.sharding import PartitionSpec as P

FACTORS = {128: (4, 4, 8), 16: (4, 1, 4)}
TILE = 8


def dot(a, b, contract):
    return lax.dot_general(a, b, (contract, ((), ())), preferred_element_type=jnp.float32)


def lat_index(z, x, y, factors):
    return (z * factors[1] + x) * factors[2] + y


def lat_coords(index, factors):
    return index // (factors[1] * factors[2]), index // factors[2] % factors[1], index % factors[2]


def groups(dims, factors):
    members = {}
    for index in range(factors[0] * factors[1] * factors[2]):
        coords = lat_coords(index, factors)
        fixed = tuple(coords[d] for d in range(3) if d not in dims)
        members.setdefault(fixed, []).append(index)
    return [members[fixed] for fixed in sorted(members)]


def swapped_core(block):
    return lax.ppermute(block, "lon", [(i, i ^ 1) for i in range(lax.axis_size("lon"))])


def paired(block, axis, first, loop):
    count = lax.axis_size(axis)
    pairs = []
    for low in range(first, count, 2):
        high = low + 1
        if high == count:
            if not loop:
                continue
            high = 0
        pairs += [(low, high), (high, low)]
    return lax.ppermute(block, axis, pairs)


def band_kernel(rows_ref, band_ref):
    count, width = rows_ref.shape
    for start in range(0, count, 2):
        pair = []
        for row in (start, start + 1):
            spread = jnp.broadcast_to(rows_ref[row : row + 1, :], (TILE, width))
            pair.append(pltpu.roll(spread, 0, 1, stride=1, stride_axis=0))
        both = jnp.concatenate(pair, axis=0).astype(jnp.bfloat16)
        band_ref[start * TILE : (start + 2) * TILE, :] = both


def feature_kernel(nbasis, tile_count, *refs):
    band_ref, cot_ref = refs[0], refs[1]
    window_refs = refs[2:9]
    features_ref, keep_ref, send_ref = refs[9:]
    rows = window_refs[0].shape[0]
    reach = band_ref.shape[1] // (7 * rows)
    per_tile = rows * TILE
    band = band_ref[...]
    for tile in range(tile_count):
        pieces = []
        for ref in window_refs:
            for row in range(rows):
                pieces.append(ref[row, tile * TILE : tile * TILE + reach, :])
        window = jnp.concatenate(pieces, axis=0)
        summed = dot(band, window, ((1,), (0,))).astype(jnp.bfloat16)
        for k in range(nbasis):
            features_ref[k, tile * per_tile : (tile + 1) * per_tile, :] = summed[
                k * per_tile : (k + 1) * per_tile
            ]
    half = cot_ref.shape[0] // 2
    channels = features_ref.shape[2]
    for k in range(nbasis):
        term = dot(cot_ref[...], features_ref[k], ((1,), (0,)))
        span = slice(k * channels, (k + 1) * channels)
        keep_ref[:, span] = term[:half].astype(keep_ref.dtype)
        send_ref[:, span] = term[half:].astype(send_ref.dtype)


def output_kernel(tile_count, features_ref, mine_ref, other_ref, order_ref, output_ref):
    nbasis, cells, channels = features_ref.shape
    rows = output_ref.shape[0]
    total = jnp.zeros((cells, order_ref.shape[0]), jnp.float32)
    for k in range(nbasis):
        span = slice(k * channels, (k + 1) * channels)
        piece = jnp.concatenate([mine_ref[:, span], other_ref[:, span]], axis=0)
        total = total + dot(features_ref[k], piece, ((1,), (1,)))
    mixed = dot(total.astype(jnp.bfloat16), order_ref[...], ((1,), (0,))).astype(jnp.bfloat16)
    for tile in range(tile_count):
        for row in range(rows):
            start = (tile * rows + row) * TILE
            output_ref[row, tile * TILE : (tile + 1) * TILE, :] = mixed[start : start + TILE]


def vmem(count):
    return [pl.BlockSpec(memory_space=pltpu.VMEM)] * count


def shards(fields, basis, spans, weight, cotangent):
    rows, cols, channels = fields.shape
    extent, nbasis, width = basis.shape[1:]
    outs = cotangent.shape[2]
    reach = (width - 1) // 2
    factors = FACTORS[lax.axis_size("lat")]
    lat = lax.axis_index("lat")
    lon = lax.axis_index("lon")
    core = lon % 2
    tile_count = cols // TILE
    window_rows = extent + rows - 1
    window_cols = TILE + width - 1
    cells = rows * cols
    bf16 = jnp.bfloat16

    offsets = jnp.arange(width) - reach
    validity = jnp.abs(offsets)[None, None, :] <= spans[:, :, None]
    masked = jnp.where(validity[:, :, None, :], basis, jnp.zeros_like(basis))
    masked = jnp.transpose(masked, (2, 0, 1, 3)).astype(jnp.float32)
    band_rows = jnp.stack(
        [
            jnp.pad(masked[:, row], ((0, 0), (row, rows - 1 - row), (0, window_cols - width)))
            for row in range(rows)
        ],
        axis=1,
    ).reshape(nbasis * rows, window_rows // rows, rows * window_cols)
    band_rows = jnp.where(lat % 2 == 0, band_rows[:, ::-1], band_rows)
    band_rows = band_rows.reshape(nbasis * rows, window_rows * window_cols)
    band = pl.pallas_call(
        band_kernel,
        out_shape=jax.ShapeDtypeStruct((nbasis * rows * TILE, window_rows * window_cols), bf16),
        in_specs=vmem(1),
        out_specs=pl.BlockSpec(memory_space=pltpu.VMEM),
    )(band_rows)

    zs, xs, ys = factors
    position = jnp.arange(outs)
    half = outs // 2
    away = (
        2
        * lat_index(
            position // ys % zs, position // (ys * zs) % xs, position % ys, factors
        )
        + (core ^ (position // half))
    )
    cot_order = (away[:, None] == jnp.arange(outs)[None, :]).astype(bf16)
    cot_cells = jnp.transpose(cotangent.reshape(rows, tile_count, TILE, outs), (1, 0, 2, 3))
    cot = dot(cot_order, cot_cells.reshape(cells, outs), ((1,), (1,))).astype(bf16)

    low, high = fields[:, :reach], fields[:, cols - reach :]
    near_edge = paired(jnp.where(core == 0, high, low), "lon", 0, True)
    far_edge = paired(jnp.where(core == 0, low, high), "lon", 1, True)
    left = jnp.where(core == 0, far_edge, near_edge)
    right = jnp.where(core == 0, near_edge, far_edge)
    own = jnp.concatenate([left, fields, right], axis=1)
    near, far = own, own
    nears, fars = [], []
    for turn in range(3):
        if turn == 2:
            near, band, cot = lax.optimization_barrier((near, band, cot))
        near, far = paired(far, "lat", 0, False), paired(near, "lat", 1, False)
        nears.append(near)
        fars.append(far)
    windows = nears[::-1] + [own] + fars

    features, keep, send = pl.pallas_call(
        lambda *refs: feature_kernel(nbasis, tile_count, *refs),
        out_shape=(
            jax.ShapeDtypeStruct((nbasis, cells, channels), bf16),
            jax.ShapeDtypeStruct((half, nbasis * channels), bf16),
            jax.ShapeDtypeStruct((half, nbasis * channels), bf16),
        ),
        in_specs=vmem(9),
        out_specs=tuple(vmem(3)),
        name="features",
    )(band, cot, *windows)

    f32 = jnp.float32
    length = nbasis * channels

    def exchanged(block, dims):
        members = groups(dims, factors)
        block = block.reshape(len(members[0]), -1, block.shape[-1])
        return lax.all_to_all(block, "lat", 0, 0, axis_index_groups=members)

    total = (keep.astype(f32) + swapped_core(send).astype(f32)).astype(bf16)
    count = zs * ys
    column = -(-length // count // 128) * 128
    mine = lax.dynamic_slice_in_dim(weight, core, 1, 0)
    folded = jnp.pad(mine, ((0, 0), (0, count * column - length))).reshape(1, count, column)
    folded = jnp.broadcast_to(folded, (xs, count, column))
    total = total.reshape(xs, count, length)
    arrived = exchanged(jnp.concatenate([total, folded], axis=2), (1,))
    total = jnp.sum(arrived[:, :, :length].astype(f32), axis=0).astype(bf16)
    gathered = arrived[:, :, length:].reshape(xs, count * column)[:, :length]

    count = zs * ys
    column = -(-length // xs // 128) * 128
    whole = jnp.broadcast_to(gathered, (count,) + gathered.shape)
    total = jnp.pad(total, ((0, 0), (0, xs * column - length))).reshape(count, xs, column)
    arrived = exchanged(jnp.concatenate([whole, total], axis=2), (0, 2))
    total = jnp.sum(arrived[:, :, length:].astype(f32), axis=0).reshape(1, -1)[:, :length]
    scale = 1.0 / math.sqrt(rows * lax.axis_size("lat") * cols * lax.axis_size("lon"))
    lon_size = lax.axis_size("lon")
    spread = jnp.broadcast_to(total * scale, (lon_size,) + total.shape)
    arrived, spread = lax.optimization_barrier((arrived, spread))
    gathered = arrived.reshape(count * xs, length + column)

    other_weight = swapped_core(gathered)
    place = position % half
    weight_row = 2 * lat_index(place // (xs * ys), place % xs, place // xs % ys, factors)
    weight_row = weight_row + (core ^ (position // half))
    weight_order = (weight_row[:, None] == jnp.arange(outs)[None, :]).astype(bf16)

    output = pl.pallas_call(
        lambda *refs: output_kernel(tile_count, *refs),
        out_shape=jax.ShapeDtypeStruct((rows, cols, outs), bf16),
        in_specs=vmem(4),
        out_specs=pl.BlockSpec(memory_space=pltpu.VMEM),
        cost_estimate=pl.CostEstimate(
            flops=2 * cells * outs * (length + outs), bytes_accessed=8 * cells * length, transcendentals=0
        ),
        name="mixing",
    )(features, gathered, other_weight, weight_order)

    arrived = lax.all_to_all(spread, "lon", 0, 0)
    arrived, output = lax.optimization_barrier((arrived, output))
    grad_weight = jnp.sum(arrived.reshape(lon_size // 2, 2, nbasis * channels), axis=0)
    return (output, grad_weight)


def solution(mesh):
    return jax.shard_map(
        shards,
        mesh=mesh,
        in_specs=(
            P("lat", "lon", None),
            P("lat", None, None, None),
            P("lat", None),
            P("lat", None),
            P("lat", "lon", None),
        ),
        out_specs=(P("lat", "lon", None), P("lat", None)),
        check_vma=False,
    )
```

```python
import math

import jax
import jax.numpy as jnp
from jax import lax
from jax.experimental import pallas as pl
from jax.experimental.pallas import tpu as pltpu
from jax.sharding import PartitionSpec as P

FACTORS = {128: (4, 4, 8), 16: (4, 1, 4)}
TILE = 8


def dot(a, b, contract):
    return lax.dot_general(a, b, (contract, ((), ())), preferred_element_type=jnp.float32)


def lat_index(z, x, y, factors):
    return (z * factors[1] + x) * factors[2] + y


def lat_coords(index, factors):
    return index // (factors[1] * factors[2]), index // factors[2] % factors[1], index % factors[2]


def groups(dims, factors):
    members = {}
    for index in range(factors[0] * factors[1] * factors[2]):
        coords = lat_coords(index, factors)
        fixed = tuple(coords[d] for d in range(3) if d not in dims)
        members.setdefault(fixed, []).append(index)
    return [members[fixed] for fixed in sorted(members)]


def swapped_core(block):
    return lax.ppermute(block, "lon", [(i, i ^ 1) for i in range(lax.axis_size("lon"))])


def paired(block, axis, first, loop):
    count = lax.axis_size(axis)
    pairs = []
    for low in range(first, count, 2):
        high = low + 1
        if high == count:
            if not loop:
                continue
            high = 0
        pairs += [(low, high), (high, low)]
    return lax.ppermute(block, axis, pairs)


def band_kernel(rows_ref, band_ref):
    count, width = rows_ref.shape
    for start in range(0, count, 2):
        pair = []
        for row in (start, start + 1):
            spread = jnp.broadcast_to(rows_ref[row : row + 1, :], (TILE, width))
            pair.append(pltpu.roll(spread, 0, 1, stride=1, stride_axis=0))
        both = jnp.concatenate(pair, axis=0).astype(jnp.bfloat16)
        band_ref[start * TILE : (start + 2) * TILE, :] = both


def feature_kernel(nbasis, tile_count, core_ref, band_ref, cot_ref, near_ref, far_ref, *refs):
    piece_refs = refs[:7]
    features_ref, keep_ref, send_ref, window_ref = refs[7:]
    rows, cols, _ = piece_refs[0].shape
    window_rows = window_ref.shape[0]
    reach = near_ref.shape[1]
    span = band_ref.shape[1] // window_rows
    per_tile = rows * TILE
    first = core_ref[0] == 0
    for row in range(window_rows):
        near, far = near_ref[row], far_ref[row]
        window_ref[row, :reach, :] = jnp.where(first, far, near)
        window_ref[row, reach : reach + cols, :] = piece_refs[row // rows][row % rows]
        window_ref[row, reach + cols :, :] = jnp.where(first, near, far)
    band = band_ref[...]
    for tile in range(tile_count):
        window = window_ref[:, tile * TILE : tile * TILE + span, :]
        window = window.reshape(window_rows * span, window.shape[2])
        summed = dot(band, window, ((1,), (0,))).astype(jnp.bfloat16)
        for k in range(nbasis):
            features_ref[k, tile * per_tile : (tile + 1) * per_tile, :] = summed[
                k * per_tile : (k + 1) * per_tile
            ]
    half = cot_ref.shape[0] // 2
    channels = features_ref.shape[2]
    for k in range(nbasis):
        term = dot(cot_ref[...], features_ref[k], ((1,), (0,)))
        span = slice(k * channels, (k + 1) * channels)
        keep_ref[:, span] = term[:half].astype(keep_ref.dtype)
        send_ref[:, span] = term[half:].astype(send_ref.dtype)


def output_kernel(tile_count, features_ref, mine_ref, other_ref, order_ref, output_ref):
    nbasis, cells, channels = features_ref.shape
    rows = output_ref.shape[0]
    total = jnp.zeros((cells, order_ref.shape[0]), jnp.float32)
    for k in range(nbasis):
        span = slice(k * channels, (k + 1) * channels)
        piece = jnp.concatenate([mine_ref[:, span], other_ref[:, span]], axis=0)
        total = total + dot(features_ref[k], piece, ((1,), (1,)))
    mixed = dot(total.astype(jnp.bfloat16), order_ref[...], ((1,), (0,))).astype(jnp.bfloat16)
    for tile in range(tile_count):
        for row in range(rows):
            start = (tile * rows + row) * TILE
            output_ref[row, tile * TILE : (tile + 1) * TILE, :] = mixed[start : start + TILE]


def vmem(count):
    return [pl.BlockSpec(memory_space=pltpu.VMEM)] * count


def shards(fields, basis, spans, weight, cotangent):
    rows, cols, channels = fields.shape
    extent, nbasis, width = basis.shape[1:]
    outs = cotangent.shape[2]
    reach = (width - 1) // 2
    factors = FACTORS[lax.axis_size("lat")]
    lat = lax.axis_index("lat")
    lon = lax.axis_index("lon")
    core = lon % 2
    tile_count = cols // TILE
    window_rows = extent + rows - 1
    window_cols = TILE + width - 1
    cells = rows * cols
    bf16 = jnp.bfloat16

    offsets = jnp.arange(width) - reach
    validity = jnp.abs(offsets)[None, None, :] <= spans[:, :, None]
    masked = jnp.where(validity[:, :, None, :], basis, jnp.zeros_like(basis))
    masked = jnp.transpose(masked, (2, 0, 1, 3)).astype(jnp.float32)
    band_rows = jnp.stack(
        [
            jnp.pad(masked[:, row], ((0, 0), (row, rows - 1 - row), (0, window_cols - width)))
            for row in range(rows)
        ],
        axis=1,
    ).reshape(nbasis * rows, window_rows // rows, rows * window_cols)
    band_rows = jnp.where(lat % 2 == 0, band_rows[:, ::-1], band_rows)
    band_rows = band_rows.reshape(nbasis * rows, window_rows * window_cols)
    band = pl.pallas_call(
        band_kernel,
        out_shape=jax.ShapeDtypeStruct((nbasis * rows * TILE, window_rows * window_cols), bf16),
        in_specs=vmem(1),
        out_specs=pl.BlockSpec(memory_space=pltpu.VMEM),
    )(band_rows)

    zs, xs, ys = factors
    position = jnp.arange(outs)
    half = outs // 2
    away = (
        2
        * lat_index(
            position // ys % zs, position // (ys * zs) % xs, position % ys, factors
        )
        + (core ^ (position // half))
    )
    cot_order = (away[:, None] == jnp.arange(outs)[None, :]).astype(bf16)
    cot_cells = jnp.transpose(cotangent.reshape(rows, tile_count, TILE, outs), (1, 0, 2, 3))
    cot = dot(cot_order, cot_cells.reshape(cells, outs), ((1,), (1,))).astype(bf16)

    near, far = fields, fields
    nears, fars = [], []
    for turn in range(3):
        if turn == 2:
            near, band, cot = lax.optimization_barrier((near, band, cot))
        near, far = paired(far, "lat", 0, False), paired(near, "lat", 1, False)
        nears.append(near)
        fars.append(far)
    pieces = nears[::-1] + [fields] + fars
    low = jnp.concatenate([piece[:, :reach] for piece in pieces], axis=0)
    high = jnp.concatenate([piece[:, cols - reach :] for piece in pieces], axis=0)
    far_edge = paired(jnp.where(core == 0, low, high), "lon", 1, True)
    near_edge = paired(jnp.where(core == 0, high, low), "lon", 0, True)

    features, keep, send = pl.pallas_call(
        lambda *refs: feature_kernel(nbasis, tile_count, *refs),
        out_shape=(
            jax.ShapeDtypeStruct((nbasis, cells, channels), bf16),
            jax.ShapeDtypeStruct((half, nbasis * channels), bf16),
            jax.ShapeDtypeStruct((half, nbasis * channels), bf16),
        ),
        in_specs=[pl.BlockSpec(memory_space=pltpu.SMEM)] + vmem(11),
        out_specs=tuple(vmem(3)),
        scratch_shapes=[pltpu.VMEM((window_rows, cols + 2 * reach, channels), bf16)],
        name="features",
    )(core.reshape(1).astype(jnp.int32), band, cot, near_edge, far_edge, *pieces)

    f32 = jnp.float32
    length = nbasis * channels

    def exchanged(block, dims):
        members = groups(dims, factors)
        block = block.reshape(len(members[0]), -1, block.shape[-1])
        return lax.all_to_all(block, "lat", 0, 0, axis_index_groups=members)

    total = (keep.astype(f32) + swapped_core(send).astype(f32)).astype(bf16)
    count = zs * ys
    column = -(-length // count // 128) * 128
    mine = lax.dynamic_slice_in_dim(weight, core, 1, 0)
    folded = jnp.pad(mine, ((0, 0), (0, count * column - length))).reshape(1, count, column)
    folded = jnp.broadcast_to(folded, (xs, count, column))
    total = total.reshape(xs, count, length)
    arrived = exchanged(jnp.concatenate([total, folded], axis=2), (1,))
    total = jnp.sum(arrived[:, :, :length].astype(f32), axis=0).astype(bf16)
    gathered = arrived[:, :, length:].reshape(xs, count * column)[:, :length]

    count = zs * ys
    column = -(-length // xs // 128) * 128
    whole = jnp.broadcast_to(gathered, (count,) + gathered.shape)
    total = jnp.pad(total, ((0, 0), (0, xs * column - length))).reshape(count, xs, column)
    arrived = exchanged(jnp.concatenate([whole, total], axis=2), (0, 2))
    total = jnp.sum(arrived[:, :, length:].astype(f32), axis=0).reshape(1, -1)[:, :length]
    scale = 1.0 / math.sqrt(rows * lax.axis_size("lat") * cols * lax.axis_size("lon"))
    lon_size = lax.axis_size("lon")
    spread = jnp.broadcast_to(total * scale, (lon_size,) + total.shape)
    arrived, spread = lax.optimization_barrier((arrived, spread))
    gathered = arrived.reshape(count * xs, length + column)

    other_weight = swapped_core(gathered)
    place = position % half
    weight_row = 2 * lat_index(place // (xs * ys), place % xs, place // xs % ys, factors)
    weight_row = weight_row + (core ^ (position // half))
    weight_order = (weight_row[:, None] == jnp.arange(outs)[None, :]).astype(bf16)

    output = pl.pallas_call(
        lambda *refs: output_kernel(tile_count, *refs),
        out_shape=jax.ShapeDtypeStruct((rows, cols, outs), bf16),
        in_specs=vmem(4),
        out_specs=pl.BlockSpec(memory_space=pltpu.VMEM),
        cost_estimate=pl.CostEstimate(
            flops=2 * cells * outs * (length + outs), bytes_accessed=8 * cells * length, transcendentals=0
        ),
        name="mixing",
    )(features, gathered, other_weight, weight_order)

    arrived = lax.all_to_all(spread, "lon", 0, 0)
    arrived, output = lax.optimization_barrier((arrived, output))
    grad_weight = jnp.sum(arrived.reshape(lon_size // 2, 2, nbasis * channels), axis=0)
    return (output, grad_weight)


def solution(mesh):
    return jax.shard_map(
        shards,
        mesh=mesh,
        in_specs=(
            P("lat", "lon", None),
            P("lat", None, None, None),
            P("lat", None),
            P("lat", None),
            P("lat", "lon", None),
        ),
        out_specs=(P("lat", "lon", None), P("lat", None)),
        check_vma=False,
    )
```
